256 devices in a mesh: src: 16 (over z_lo, y), tgt: 16 (over x, z_hi, core).
Axes of the slice: x: 4, y: 4, z: 8 (z_hi: 2, z_lo: 4; z = z_hi * 4 + z_lo), core: 2. Of those that a mesh axis runs over, the one named last changes fastest.
Arguments:
- signals: float32 [64, 786432], P(None, ('src', 'tgt')), may hold values from -6 to 6
- leaf_maps: float32 [6144, 64, 128], P(('src', 'tgt')), may hold values from -0.5 to 0.5
- root_maps: float32 [6144, 128, 64], P(('src', 'tgt')), may hold values from -0.75 to 0.75
- translations: float32 [8, 8, 64, 64], replicated, may hold values from -0.375 to 0.375
- source_list: int32 [8, 24, 4], replicated, may hold values from 0 to 47, as said below
- type_list: int32 [8, 24, 4], replicated, may hold values from 0 to 7
Outputs:
- focused: float32 [64, 786432], P(None, ('src', 'tgt'))
The draws below stay inside these ranges and needn't reach their ends.
Inputs may be any that keep to these rules, and one draw needn't show every extreme that they name: `source_list`: entries e < 2 name one of the device's own blocks (below 24); the other entries name one of the partner's blocks (at or above 24).
All inputs are finite; a program needn't handle non-finite values.
Results may differ from the reference program's by a relative error of at most 0.00011.
Values sent between devices are 32-bit elements; how exact they have to be, the bound alone decides.
No kernel may reach another device: no remote copies, remote signals or barrier semaphores. Data moves between devices by JAX's collectives and lax.ppermute only.
A program may use at most 64 MiB of HBM per device.

```python
import jax
import jax.numpy as jnp
import numpy as np
from jax import lax

W = 64
R = 64
BS = 128
KB = 24
DEG = 4
NT = 8
LEVELS = 8
NB = 6144
N_EL = 786432
N_SRC = 16
N_TGT = 16


def draw_source_list(key, part):
    key_base = jax.random.fold_in(key, 11)
    key_low = jax.random.fold_in(key, 12)
    key_high = jax.random.fold_in(key, 13)
    base = jax.random.randint(key_base, (LEVELS, KB, DEG), 0, KB)
    entry = jax.lax.broadcasted_iota(jnp.int32, (LEVELS, KB, DEG), 2)
    block = jax.lax.broadcasted_iota(jnp.int32, (LEVELS, KB, DEG), 1)
    low_pick = jax.random.randint(key_low, (LEVELS, 1, 1), 0, KB)
    high_pick = jax.random.randint(key_high, (LEVELS, 1, 1), 0, KB)
    base = jnp.where((block == low_pick) & (entry == 0), 0, base)
    base = jnp.where((block == high_pick) & (entry == DEG - 1), KB - 1, base)
    offset = jnp.where(entry >= DEG // 2, KB, 0)
    return (base + offset).astype(jnp.int32)


def touch_ends(entries, stream_key, least, top_value):
    shape = entries.shape
    spot = [jax.random.randint(jax.random.fold_in(stream_key, axis), (), 0, shape[axis]) for axis in range(len(shape))]
    entries = entries.at[tuple(spot)].set(least)
    longest = shape.index(max(shape))
    spot[longest] = (spot[longest] + 1) % shape[longest]
    return entries.at[tuple(spot)].set(top_value)


def levels(key, dims, cuts, smallest, top_value):
    def one(position, shards_of):
        steps = jax.random.uniform(jax.random.fold_in(jax.random.fold_in(key, 6), position), (shards_of,), jnp.float32, smallest / len(cuts), top_value / len(cuts))
        return jnp.repeat(jnp.exp(steps), dims[position] // shards_of).reshape((-1,) + (1,) * (len(dims) - position - 1))

    gain = one(*cuts[0])
    for cut in cuts[1:]:
        gain = gain * one(*cut)
    return gain


def bell_draw(rng, extent, deviation, most, split=(), kind=jnp.bfloat16):
    entries = jax.random.normal(rng, extent, jnp.float32) * deviation
    if len(split) > 0:
        entries = levels(rng, extent, split, -0.22, 0.18) * entries
    return jnp.clip(entries, min=-most, max=most).astype(kind)


def setup_inputs(seed: int = 0) -> dict:
    splits = jax.random.split(jax.random.key(seed), 7)
    signals = bell_draw(splits[0], (W, N_EL), 1.0, 6.0, ((1, 256),), jnp.float32)
    leaf_maps = bell_draw(splits[1], (NB, R, BS), BS ** -0.5, 0.5, ((0, 256),), jnp.float32)
    root_maps = bell_draw(splits[2], (NB, BS, R), R ** -0.5, 0.75, ((0, 256),), jnp.float32)
    translations = bell_draw(splits[3], (LEVELS, NT, R, R), (DEG * R) ** -0.5, 0.375, (), jnp.float32)
    source_list = draw_source_list(jax.random.fold_in(splits[6], 71), 0)
    type_list = touch_ends(jax.random.randint(splits[5], (LEVELS, KB, DEG), 0, NT), jax.random.fold_in(splits[5], 1), 0, NT - 1).astype(jnp.int32)
    return dict(signals=signals, leaf_maps=leaf_maps, root_maps=root_maps, translations=translations, source_list=source_list, type_list=type_list)


HIGH = lax.Precision.HIGHEST


def flip_along(coef, axis, count, bit):
    order = np.arange(count) ^ (1 << bit)
    return jnp.take(coef, jnp.asarray(order, dtype=jnp.int32), axis=axis)


def reference(signals, leaf_maps, root_maps, translations, source_list, type_list):
    grouped = signals.reshape(W, NB, BS)
    coef = jnp.einsum('grb,wgb->grw', leaf_maps, grouped, precision=HIGH)
    coef = coef.reshape(N_SRC, N_TGT, KB, R, W)
    src_bits = int(N_SRC).bit_length() - 1
    tgt_bits = int(N_TGT).bit_length() - 1
    for level in range(LEVELS):
        if level < LEVELS // 2:
            partner = flip_along(coef, 0, N_SRC, level % src_bits)
        else:
            partner = flip_along(coef, 1, N_TGT, (level - LEVELS // 2) % tgt_bits)
        stack = jnp.concatenate([coef, partner], axis=2)
        total = jnp.zeros((N_SRC, N_TGT, KB, R, W), jnp.float32)
        for entry in range(DEG):
            mats = translations[level][type_list[level, :, entry]]
            picked = jnp.take(stack, source_list[level, :, entry].astype(jnp.int32), axis=2)
            total = total + jnp.einsum('krs,abksw->abkrw', mats, picked, precision=HIGH)
        coef = total
    flat = coef.reshape(NB, R, W)
    focused = jnp.einsum('gbr,grw->wgb', root_maps, flat, precision=HIGH)
    return focused.reshape(W, N_EL)
```

```python
import functools

import jax
import jax.numpy as jnp
from jax import lax
from jax.experimental import pallas as pl
from jax.experimental.pallas import tpu as pltpu
from jax.sharding import Mesh, PartitionSpec as P

BITS = ("z1", "z0", "y1", "y0", "x1", "x0", "zh", "c")
PLANE = ("y1", "y0", "x1", "x0", "c")
COLUMN = ("z1", "z0", "zh")
LANES = 128
F32, BF16 = jnp.float32, jnp.bfloat16
NT = (((1,), (1,)), ((), ()))


def dot_nt(a, b):
    return lax.dot_general(a, b, NT, preferred_element_type=F32)


def split(x):
    hi = x.astype(BF16)
    return hi, (x - hi.astype(F32)).astype(BF16)


def low_lanes(shape):
    return lax.broadcasted_iota(jnp.int32, shape, 1) < LANES // 2


def hi_lo_lanes(x):
    hi = x.astype(BF16).astype(F32)
    return jnp.where(low_lanes(x.shape), hi, x - hi).astype(BF16)


def flip_rows(v, mask):
    groups = [v[8 * i : 8 * i + 8] for i in range(v.shape[0] // 8)]
    if mask >= 8:
        groups = [groups[i ^ (mask // 8)] for i in range(len(groups))]
    elif mask == 4:
        groups = [pltpu.roll(g, 4, 0) for g in groups]
    else:
        bit = (lax.broadcasted_iota(jnp.int32, (8, LANES), 0) & mask) != 0
        groups = [jnp.where(bit, pltpu.roll(g, mask, 0), pltpu.roll(g, 8 - mask, 0)) for g in groups]
    return jnp.concatenate(groups, axis=0)


def put_pair(held, pair, x):
    turned = pltpu.roll(x, LANES // 2, 1)
    low = low_lanes(x.shape)
    held[2 * pair] = hi_lo_lanes(jnp.where(low, x, turned))
    held[2 * pair + 1] = hi_lo_lanes(jnp.where(low, turned, x))


def level_step(level, mask, held, products, table, sources, types, emit):
    blocks, rows = held.shape[0], held.shape[1]
    kinds, rank = table.shape[0], table.shape[1]
    mats = table[...].reshape(kinds * rank, rank)
    mats = jnp.concatenate([mats, mats], axis=1)
    mats_hi, mats_lo = split(mats)
    weights = jnp.concatenate([mats_hi, mats_lo], axis=1)
    step = 4

    def multiply(i, carry):
        left = held[pl.ds(i * step, step)].reshape(step * rows, LANES)
        left = jnp.concatenate([left, left], axis=1)
        out = dot_nt(left, weights)
        for j in range(step):
            for t in range(kinds // 2):
                products[i * step + j, t] = out[j * rows : (j + 1) * rows, t * LANES : (t + 1) * LANES]
        return carry

    lax.fori_loop(0, blocks // step, multiply, 0, unroll=2)
    entries = 4
    upper = jnp.where(low_lanes((rows, LANES)), 0, 1)

    def gathered(block):
        def term(e):
            at = (level * blocks + block) * entries + e
            kind = types[at]
            source = sources[at] - (blocks if e >= entries // 2 else 0)
            value = products[source, kind // 2]
            return jnp.where(upper == kind % 2, value, 0.0)

        own = term(0) + term(1)
        other = term(2) + term(3)
        total = own + flip_rows(other, mask)
        return total + pltpu.roll(total, LANES // 2, 1)

    def combine(pair, carry):
        even, odd = gathered(2 * pair), gathered(2 * pair + 1)
        emit(pair, even, odd)
        return carry

    lax.fori_loop(0, blocks // 2, combine, 0, unroll=2)


def levels_kernel(first, masks, get, sources, types, tables, x_ref, out_ref, held, products):
    blocks = held.shape[0]

    def take(pair, carry):
        put_pair(held, pair, get(x_ref, pair))
        return carry

    lax.fori_loop(0, blocks // 2, take, 0, unroll=2)

    def keep(pair, even, odd):
        held[2 * pair] = hi_lo_lanes(even)
        held[2 * pair + 1] = hi_lo_lanes(odd)

    def give(pair, even, odd):
        lanes = pl.ds(pl.multiple_of(pair * LANES, LANES), LANES)
        out_ref[:, lanes] = jnp.where(low_lanes(even.shape), even, odd)

    for i, mask in enumerate(masks):
        emit = give if i == len(masks) - 1 else keep
        level_step(first + i, mask, held, products, tables.at[i], sources, types, emit)


def get_plane(x_ref, pair):
    pairs = 12
    parts = []
    for y in range(4):
        for half in range(2):
            parts.append(x_ref[pl.ds((y * 16 + half) * pairs + pair, 8, stride=2 * pairs), :])
    return jnp.concatenate(parts, axis=0)


def get_column(x_ref, pair):
    return x_ref[:, pl.ds(pl.multiple_of(pair * LANES, LANES), LANES)]


def leaf_kernel(signals, maps, out_ref):
    pairs = maps.shape[0] // 2
    width = maps.shape[2]
    rows = signals.shape[0]

    def one(k):
        wave_hi, wave_lo = split(signals[:, pl.ds(pl.multiple_of(k * width, width), width)])
        map_hi, map_lo = split(maps[k])
        left = jnp.concatenate([wave_hi, wave_lo], axis=1)
        right = jnp.concatenate([map_hi, map_hi], axis=1)
        return dot_nt(left, right) + dot_nt(wave_hi, map_lo)

    def body(pair, carry):
        out_ref[pl.ds(pair, rows, stride=pairs), :] = jnp.concatenate([one(2 * pair), one(2 * pair + 1)], axis=1)
        return carry

    lax.fori_loop(0, pairs, body, 0, unroll=3)


def order_kernel(x_ref, out_ref):
    pairs = 12
    for pair in range(pairs):
        for y in range(4):
            for half in range(2):
                rows = pl.ds((y * 16 + half) * pairs + pair, 8, stride=2 * pairs)
                out_ref[rows, :] = x_ref[(y * 2 + half) * 8 : (y * 2 + half) * 8 + 8, pair * LANES : (pair + 1) * LANES]


def root_kernel(x_ref, maps, out_ref):
    pairs = maps.shape[0] // 2
    rank, width = maps.shape[1], maps.shape[2]
    rows = out_ref.shape[0]

    def body(pair, carry):
        coef_hi, coef_lo = split(x_ref[pl.ds(pair, rows, stride=pairs), :])
        none = jnp.zeros((rank, width), BF16)
        even_hi, even_lo = split(maps[2 * pair])
        odd_hi, odd_lo = split(maps[2 * pair + 1])

        def both(even, odd):
            even, odd = jnp.concatenate([even, none], axis=1), jnp.concatenate([none, odd], axis=1)
            return jnp.concatenate([even, odd], axis=0)

        map_hi, map_lo = both(even_hi, odd_hi), both(even_lo, odd_lo)
        left = jnp.concatenate([coef_hi, coef_lo], axis=1)
        right = jnp.concatenate([map_hi, map_hi], axis=0)
        out = jnp.dot(left, right, preferred_element_type=F32) + jnp.dot(coef_hi, map_lo, preferred_element_type=F32)
        out_ref[:, pl.ds(pl.multiple_of(pair * 2 * width, 2 * width), 2 * width)] = out
        return carry

    lax.fori_loop(0, pairs, body, 0, unroll=2)


VMEM = pl.BlockSpec(memory_space=pltpu.VMEM)
SMEM = pl.BlockSpec(memory_space=pltpu.SMEM)


def call(kernel, shape, specs, scratch=()):
    return pl.pallas_call(
        kernel,
        out_shape=jax.ShapeDtypeStruct(shape, F32),
        in_specs=specs,
        out_specs=VMEM,
        scratch_shapes=scratch,
        compiler_params=pltpu.CompilerParams(vmem_limit_bytes=60 * 2**20),
    )


def exchange(x, axes):
    return lax.all_to_all(x, axes, 0, 0, tiled=True)


def local(signals, leaf_maps, root_maps, translations, source_list, type_list):
    blocks, rank, width = leaf_maps.shape
    waves = signals.shape[0]
    pairs = blocks // 2
    kinds = translations.shape[1]
    sources, types = source_list.reshape(-1), type_list.reshape(-1)
    scratch = [pltpu.VMEM((blocks, waves, LANES), BF16), pltpu.VMEM((blocks, kinds // 2, waves, LANES), F32)]
    flat, wide = (waves * pairs, LANES), (waves, pairs * LANES)
    specs = [SMEM, SMEM, VMEM, VMEM]

    x = call(leaf_kernel, flat, [VMEM, VMEM])(signals, leaf_maps)
    x = exchange(x.reshape(32, waves * pairs // 32, LANES), PLANE).reshape(flat)
    x = call(functools.partial(levels_kernel, 0, (16, 32), get_plane), wide, specs, scratch)(
        sources, types, translations[:2], x
    )
    x = exchange(x.reshape(8, waves // 8, pairs * LANES), COLUMN).reshape(wide)
    x = call(functools.partial(levels_kernel, 2, (16, 32, 1, 8, 2, 4), get_column), wide, specs, scratch)(
        sources, types, translations[2:], x
    )
    x = exchange(x.reshape(8, waves // 8, pairs * LANES), COLUMN).reshape(wide)
    x = call(order_kernel, flat, [VMEM])(x)
    x = exchange(x.reshape(32, waves * pairs // 32, LANES), PLANE).reshape(flat)
    return call(root_kernel, (waves, blocks * width), [VMEM, VMEM])(x, jnp.swapaxes(root_maps, 1, 2))


def solution(mesh):
    fine = Mesh(mesh.devices.reshape((2,) * len(BITS)), BITS)
    placed = (P(None, BITS), P(BITS, None, None), P(BITS, None, None), P(), P(), P())
    return jax.shard_map(local, mesh=fine, in_specs=placed, out_specs=P(None, BITS), check_vma=False)
```

```python
import functools

import jax
import jax.numpy as jnp
from jax import lax
from jax.experimental import pallas as pl
from jax.experimental.pallas import tpu as pltpu
from jax.sharding import Mesh, PartitionSpec as P

BITS = ("z1", "z0", "y1", "y0", "x1", "x0", "zh", "c")
GROUP = ("z1", "z0", "y1", "x1", "x0", "zh")
FLIPS = ("y0", "y1", "z0", "z1", "c", "zh", "x0", "x1")
LANES = 128
F32, BF16 = jnp.float32, jnp.bfloat16
NT = (((1,), (1,)), ((), ()))


def row_mask(level):
    return 1 << (len(GROUP) - 1 - GROUP.index(FLIPS[level]))


def dot_nt(a, b):
    return lax.dot_general(a, b, NT, preferred_element_type=F32)


def split(x):
    hi = x.astype(BF16)
    return hi, (x - hi.astype(F32)).astype(BF16)


def low_lanes(shape):
    return lax.broadcasted_iota(jnp.int32, shape, 1) < LANES // 2


def turn(x):
    return pltpu.roll(x, LANES // 2, 1)


def hi_lo_lanes(x):
    hi = x.astype(BF16).astype(F32)
    return jnp.where(low_lanes(x.shape), hi, x - hi).astype(BF16)


def flip_rows(v, mask):
    groups = [v[8 * i : 8 * i + 8] for i in range(v.shape[0] // 8)]
    if mask >= 8:
        groups = [groups[i ^ (mask // 8)] for i in range(len(groups))]
    elif mask == 4:
        groups = [pltpu.roll(g, 4, 0) for g in groups]
    else:
        bit = (lax.broadcasted_iota(jnp.int32, (8, LANES), 0) & mask) != 0
        groups = [jnp.where(bit, pltpu.roll(g, mask, 0), pltpu.roll(g, 8 - mask, 0)) for g in groups]
    return jnp.concatenate(groups, axis=0)


def pair_rows(ref, pair):
    return pl.ds(pair, ref.shape[0] // 12, stride=12)


def put_pair(held, pair, x):
    turned = turn(x)
    low = low_lanes(x.shape)
    held[2 * pair] = hi_lo_lanes(jnp.where(low, x, turned))
    held[2 * pair + 1] = hi_lo_lanes(jnp.where(low, turned, x))


def put_weights(mat, out_ref):
    hi, lo = split(mat.T)
    both = jnp.concatenate([hi, lo], axis=1)
    rank = mat.shape[0]
    out_ref[:rank] = both
    out_ref[rank:] = both


def two_terms(level, block, entry, sources, types, back, held, weights):
    left = [held[sources[level, entry + i, block] - back] for i in range(2)]
    right = [weights[types[level, entry + i, block]] for i in range(2)]
    return jnp.dot(jnp.concatenate(left, axis=1), jnp.concatenate(right, axis=0), preferred_element_type=F32)


def level_step(level, sources, types, held, weights, emit):
    blocks = held.shape[0]

    def pair_step(pair, carry):
        terms = []
        for block in (2 * pair, 2 * pair + 1):
            terms.append(two_terms(level, block, 0, sources, types, 0, held, weights))
            terms.append(two_terms(level, block, 2, sources, types, blocks, held, weights))
        emit(pair, *terms)
        return carry

    lax.fori_loop(0, blocks // 2, pair_step, 0, unroll=6)


def flip_and_keep(held, mask):
    def emit(pair, own_even, other_even, own_odd, other_odd):
        for block, own, other in ((2 * pair, own_even, other_even), (2 * pair + 1, own_odd, other_odd)):
            total = own + flip_rows(other, mask)
            held[block] = hi_lo_lanes(total + turn(total))

    return emit


def flip_and_give(out_ref, mask):
    def emit(pair, own_even, other_even, own_odd, other_odd):
        even = own_even + flip_rows(other_even, mask)
        odd = own_odd + flip_rows(other_odd, mask)
        out_ref[pair_rows(out_ref, pair), :] = join(even, odd)

    return emit


def join(even, odd):
    low = low_lanes(even.shape)
    return jnp.where(low, even, odd) + turn(jnp.where(low, odd, even))


def give_both(own_ref, other_ref):
    def emit(pair, own_even, other_even, own_odd, other_odd):
        own_ref[pair_rows(own_ref, pair), :] = join(own_even, own_odd)
        other_ref[pair_rows(other_ref, pair), :] = join(other_even, other_odd)

    return emit


def run_levels(first, count, sources, types, held, weights, last):
    for i in range(count):
        now, then = held[i % 2], held[(i + 1) % 2]
        emit = last if i == count - 1 else flip_and_keep(then, row_mask(first + i))
        level_step(first + i, sources, types, now, weights.at[first + i - 1], emit)


def start_kernel(
    sources, types, tables, signals, maps, own_ref, other_ref, held, weights, table_in, signals_in, maps_in, sems
):
    blocks, rank, width = maps.shape
    parts = sems.shape[1]
    some = blocks // parts
    table_copy = pltpu.make_async_copy(tables.at[0], table_in, sems.at[2, 0])
    table_copy.start()
    copies = []
    for i in range(parts):
        lanes, rows = pl.ds(i * some * width, some * width), pl.ds(i * some, some)
        copies.append(
            (
                pltpu.make_async_copy(signals.at[:, lanes], signals_in.at[:, lanes], sems.at[0, i]),
                pltpu.make_async_copy(maps.at[rows], maps_in.at[rows], sems.at[1, i]),
            )
        )
        for copy in copies[-1]:
            copy.start()
    table_copy.wait()
    for kind in range(weights.shape[0]):
        put_weights(table_in[kind], weights.at[kind])

    def leaf(k, carry):
        wave_hi, wave_lo = split(signals_in[:, pl.ds(pl.multiple_of(k * width, width), width)])
        map_hi, map_lo = split(maps_in[k])
        left = jnp.concatenate([wave_hi, wave_lo], axis=1)
        both = jnp.concatenate([map_hi, map_lo], axis=0)
        total = dot_nt(left, jnp.concatenate([both, both], axis=1))
        held[k] = hi_lo_lanes(total + turn(total))
        return carry

    for i in range(parts):
        for copy in copies[i]:
            copy.wait()
        lax.fori_loop(i * some, (i + 1) * some, leaf, 0, unroll=some)
    level_step(0, sources, types, held, weights, give_both(own_ref, other_ref))


def prepare_kernel(tables, maps, weights, root_weights):
    def table(level, carry):
        for kind in range(tables.shape[1]):
            put_weights(tables[level + 1, kind], weights.at[level, kind])
        return carry

    lax.fori_loop(0, tables.shape[0] - 1, table, 0)

    def root(block, carry):
        hi, lo = split(maps[block])
        root_weights[block] = jnp.concatenate([hi, hi, lo, lo], axis=0)
        return carry

    lax.fori_loop(0, maps.shape[0], root, 0, unroll=4)


def middle_kernel(sources, types, weights, x_ref, own_ref, other_ref, held, held_too):
    for pair in range(held.shape[0] // 2):
        put_pair(held, pair, x_ref[pair_rows(x_ref, pair), :])
    run_levels(1, 4, sources, types, (held, held_too), weights, give_both(own_ref, other_ref))


def end_kernel(sources, types, weights, own_ref, other_ref, out_ref, held, held_too):
    for pair in range(held.shape[0] // 2):
        rows = pair_rows(own_ref, pair)
        put_pair(held, pair, own_ref[rows, :] + other_ref[rows, :])
    run_levels(5, 3, sources, types, (held, held_too), weights, flip_and_give(out_ref, row_mask(7)))


def root_kernel(x_ref, weights, out_ref):
    blocks, width = weights.shape[0], weights.shape[2]

    def body(pair, carry):
        x = x_ref[pair_rows(x_ref, pair), :]
        turned = turn(x)
        low = low_lanes(x.shape)
        for block, value in ((2 * pair, jnp.where(low, x, turned)), (2 * pair + 1, jnp.where(low, turned, x))):
            left = hi_lo_lanes(value)
            out = jnp.dot(jnp.concatenate([left, left], axis=1), weights[block], preferred_element_type=F32)
            out_ref[:, pl.ds(pl.multiple_of(block * width, width), width)] = out
        return carry

    lax.fori_loop(0, blocks // 2, body, 0, unroll=4)


VMEM = pl.BlockSpec(memory_space=pltpu.VMEM)
SMEM = pl.BlockSpec(memory_space=pltpu.SMEM)
HBM = pl.BlockSpec(memory_space=pltpu.HBM)


def call(kernel, outs, specs, scratch=(), mib=12, cost=None):
    return pl.pallas_call(
        kernel,
        out_shape=outs,
        grid=(1,),
        in_specs=specs,
        out_specs=[VMEM] * len(outs),
        scratch_shapes=scratch,
        cost_estimate=cost,
        compiler_params=pltpu.CompilerParams(vmem_limit_bytes=mib * 2**20),
    )


def exchange(x):
    rows = x.shape[0]
    x = x.reshape(64, 1, rows * LANES // 64)
    return lax.all_to_all(x, GROUP, 0, 0, tiled=True).reshape(rows, LANES)


def partner(x, axis):
    return lax.ppermute(x, axis, [(0, 1), (1, 0)])


def local(signals, leaf_maps, root_maps, translations, source_list, type_list):
    blocks, rank, width = leaf_maps.shape
    waves = signals.shape[0]
    levels, kinds = translations.shape[:2]
    sources, types = jnp.swapaxes(source_list, 1, 2), jnp.swapaxes(type_list, 1, 2)
    root_maps = jnp.swapaxes(root_maps, 1, 2)
    held = pltpu.VMEM((blocks, waves, LANES), BF16)
    flat = jax.ShapeDtypeStruct((waves * blocks // 2, LANES), F32)
    own, other = call(
        start_kernel,
        [flat, flat],
        [SMEM, SMEM, HBM, HBM, HBM],
        [
            held,
            pltpu.VMEM((kinds, 2 * rank, LANES), BF16),
            pltpu.VMEM((kinds, rank, rank), F32),
            pltpu.VMEM((waves, blocks * width), F32),
            pltpu.VMEM((blocks, rank, width), F32),
            pltpu.SemaphoreType.DMA((3, 3)),
        ],
        mib=60,
    )(sources, types, translations, signals, leaf_maps)
    received = partner(other, "y0")
    weights, root_weights = call(
        prepare_kernel,
        [
            jax.ShapeDtypeStruct((levels - 1, kinds, 2 * rank, LANES), BF16),
            jax.ShapeDtypeStruct((blocks, 4 * rank, width), BF16),
        ],
        [VMEM, VMEM],
        cost=pl.CostEstimate(flops=2**24, bytes_accessed=2**23, transcendentals=0),
    )(translations, root_maps)
    x, weights, root_weights = lax.optimization_barrier((own + received, weights, root_weights))
    x = exchange(x)
    own, other = call(middle_kernel, [flat, flat], [SMEM, SMEM, VMEM, VMEM], [held, held])(sources, types, weights, x)
    (x,) = call(end_kernel, [flat], [SMEM, SMEM, VMEM, VMEM, VMEM], [held, held])(
        sources, types, weights, own, partner(other, "c")
    )
    (out,) = call(root_kernel, [jax.ShapeDtypeStruct((waves, blocks * width), F32)], [VMEM, VMEM])(
        exchange(x), root_weights
    )
    return out


def solution(mesh):
    fine = Mesh(mesh.devices.reshape((2,) * len(BITS)), BITS)
    placed = (P(None, BITS), P(BITS, None, None), P(BITS, None, None), P(), P(), P())
    return jax.shard_map(local, mesh=fine, in_specs=placed, out_specs=P(None, BITS), check_vma=False)
```

```python
import functools

import jax
import jax.numpy as jnp
from jax import lax
from jax.experimental import pallas as pl
from jax.experimental.pallas import tpu as pltpu
from jax.sharding import Mesh, PartitionSpec as P

BITS = ("z1", "z0", "y1", "y0", "x1", "x0", "zh", "c")
GROUP = ("z1", "z0", "y1", "x1", "x0", "zh")
FOLDED = "y0"
FLIPS = ("y0", "y1", "z0", "z1", "c", "zh", "x0", "x1")
LANES = 128
F32, BF16 = jnp.float32, jnp.bfloat16
NT = (((1,), (1,)), ((), ()))


def row_mask(level):
    return 1 << (len(GROUP) - 1 - GROUP.index(FLIPS[level]))


def dot_nt(a, b):
    return lax.dot_general(a, b, NT, preferred_element_type=F32)


def split(x):
    hi = x.astype(BF16)
    return hi, (x - hi.astype(F32)).astype(BF16)


def low_lanes(shape):
    return lax.broadcasted_iota(jnp.int32, shape, 1) < LANES // 2


def turn(x):
    return pltpu.roll(x, LANES // 2, 1)


def hi_lo_lanes(x):
    hi = x.astype(BF16).astype(F32)
    return jnp.where(low_lanes(x.shape), hi, x - hi).astype(BF16)


def flip_rows(v, mask):
    groups = [v[8 * i : 8 * i + 8] for i in range(v.shape[0] // 8)]
    if mask >= 8:
        groups = [groups[i ^ (mask // 8)] for i in range(len(groups))]
    elif mask == 4:
        groups = [pltpu.roll(g, 4, 0) for g in groups]
    else:
        bit = (lax.broadcasted_iota(jnp.int32, (8, LANES), 0) & mask) != 0
        groups = [jnp.where(bit, pltpu.roll(g, mask, 0), pltpu.roll(g, 8 - mask, 0)) for g in groups]
    return jnp.concatenate(groups, axis=0)


def pair_rows(ref, pair, first=0):
    return pl.ds(first * 12 + pair, 64, stride=12)


def put_pair(held, pair, x):
    turned = turn(x)
    low = low_lanes(x.shape)
    held[2 * pair] = hi_lo_lanes(jnp.where(low, x, turned))
    held[2 * pair + 1] = hi_lo_lanes(jnp.where(low, turned, x))


def put_weights(mat, out_ref):
    hi, lo = split(mat.T)
    both = jnp.concatenate([hi, lo], axis=1)
    rank = mat.shape[0]
    out_ref[:rank] = both
    out_ref[rank:] = both


def two_terms(level, block, entry, sources, types, back, held, weights):
    left = [held[sources[level, entry + i, block] - back] for i in range(2)]
    right = [weights[types[level, entry + i, block]] for i in range(2)]
    return jnp.dot(jnp.concatenate(left, axis=1), jnp.concatenate(right, axis=0), preferred_element_type=F32)


def level_step(level, sources, types, held, weights, emit):
    blocks = held.shape[0]

    def pair_step(pair, carry):
        terms = []
        for block in (2 * pair, 2 * pair + 1):
            terms.append(two_terms(level, block, 0, sources, types, 0, held, weights))
            terms.append(two_terms(level, block, 2, sources, types, blocks, held, weights))
        emit(pair, *terms)
        return carry

    lax.fori_loop(0, blocks // 2, pair_step, 0, unroll=6)


def flip_and_keep(held, mask):
    def emit(pair, own_even, other_even, own_odd, other_odd):
        for block, own, other in ((2 * pair, own_even, other_even), (2 * pair + 1, own_odd, other_odd)):
            total = own + flip_rows(other, mask)
            held[block] = hi_lo_lanes(total + turn(total))

    return emit


def flip_and_give(out_ref, mask):
    def emit(pair, own_even, other_even, own_odd, other_odd):
        even = own_even + flip_rows(other_even, mask)
        odd = own_odd + flip_rows(other_odd, mask)
        out_ref[pair_rows(out_ref, pair), :] = join(even, odd)

    return emit


def join(even, odd):
    low = low_lanes(even.shape)
    return jnp.where(low, even, odd) + turn(jnp.where(low, odd, even))


def give_both(own_ref, other_ref):
    def emit(pair, own_even, other_even, own_odd, other_odd):
        own_ref[pair_rows(own_ref, pair), :] = join(own_even, own_odd)
        other_ref[pair_rows(other_ref, pair), :] = join(other_even, other_odd)

    return emit


def give_by_bit(mine, out_ref):
    def emit(pair, own_even, other_even, own_odd, other_odd):
        own, other = join(own_even, own_odd), join(other_even, other_odd)
        out_ref[pair_rows(out_ref, pair), :] = jnp.where(mine == 0, own, other)
        out_ref[pair_rows(out_ref, pair, 64), :] = jnp.where(mine == 0, other, own)

    return emit


def run_levels(first, count, sources, types, held, weights, last):
    for i in range(count):
        now, then = held[i % 2], held[(i + 1) % 2]
        emit = last if i == count - 1 else flip_and_keep(then, row_mask(first + i))
        level_step(first + i, sources, types, now, weights.at[first + i - 1], emit)


def start_kernel(
    sources, types, mine, tables, signals, maps, out_ref, held, weights, table_in, signals_in, maps_in, sems
):
    blocks, rank, width = maps.shape
    parts = sems.shape[1]
    some = blocks // parts
    table_copy = pltpu.make_async_copy(tables.at[0], table_in, sems.at[2, 0])
    table_copy.start()
    copies = []
    for i in range(parts):
        lanes, rows = pl.ds(i * some * width, some * width), pl.ds(i * some, some)
        copies.append(
            (
                pltpu.make_async_copy(signals.at[:, lanes], signals_in.at[:, lanes], sems.at[0, i]),
                pltpu.make_async_copy(maps.at[rows], maps_in.at[rows], sems.at[1, i]),
            )
        )
        for copy in copies[-1]:
            copy.start()
    table_copy.wait()
    for kind in range(weights.shape[0]):
        put_weights(table_in[kind], weights.at[kind])

    def leaf(k, carry):
        wave_hi, wave_lo = split(signals_in[:, pl.ds(pl.multiple_of(k * width, width), width)])
        map_hi, map_lo = split(maps_in[k])
        left = jnp.concatenate([wave_hi, wave_lo], axis=1)
        both = jnp.concatenate([map_hi, map_lo], axis=0)
        total = dot_nt(left, jnp.concatenate([both, both], axis=1))
        held[k] = hi_lo_lanes(total + turn(total))
        return carry

    for i in range(parts):
        for copy in copies[i]:
            copy.wait()
        lax.fori_loop(i * some, (i + 1) * some, leaf, 0, unroll=some)
    level_step(0, sources, types, held, weights, give_by_bit(mine[0], out_ref))


def prepare_kernel(tables, maps, weights, root_weights):
    def table(level, carry):
        for kind in range(tables.shape[1]):
            put_weights(tables[level + 1, kind], weights.at[level, kind])
        return carry

    lax.fori_loop(0, tables.shape[0] - 1, table, 0)

    def root(block, carry):
        hi, lo = split(maps[block])
        root_weights[block] = jnp.concatenate([hi, hi, lo, lo], axis=0)
        return carry

    lax.fori_loop(0, maps.shape[0], root, 0, unroll=4)


def middle_kernel(sources, types, weights, x_ref, own_ref, other_ref, held, held_too):
    for pair in range(held.shape[0] // 2):
        put_pair(held, pair, x_ref[pair_rows(x_ref, pair), :] + x_ref[pair_rows(x_ref, pair, 64), :])
    run_levels(1, 4, sources, types, (held, held_too), weights, give_both(own_ref, other_ref))


def end_kernel(sources, types, weights, own_ref, other_ref, out_ref, held, held_too):
    for pair in range(held.shape[0] // 2):
        rows = pair_rows(own_ref, pair)
        put_pair(held, pair, own_ref[rows, :] + other_ref[rows, :])
    run_levels(5, 3, sources, types, (held, held_too), weights, flip_and_give(out_ref, row_mask(7)))


def root_kernel(x_ref, weights, out_ref):
    blocks, width = weights.shape[0], weights.shape[2]

    def body(pair, carry):
        x = x_ref[pair_rows(x_ref, pair), :]
        turned = turn(x)
        low = low_lanes(x.shape)
        for block, value in ((2 * pair, jnp.where(low, x, turned)), (2 * pair + 1, jnp.where(low, turned, x))):
            left = hi_lo_lanes(value)
            out = jnp.dot(jnp.concatenate([left, left], axis=1), weights[block], preferred_element_type=F32)
            out_ref[:, pl.ds(pl.multiple_of(block * width, width), width)] = out
        return carry

    lax.fori_loop(0, blocks // 2, body, 0, unroll=4)


VMEM = pl.BlockSpec(memory_space=pltpu.VMEM)
SMEM = pl.BlockSpec(memory_space=pltpu.SMEM)
HBM = pl.BlockSpec(memory_space=pltpu.HBM)


def call(kernel, outs, specs, scratch=(), mib=12, cost=None):
    return pl.pallas_call(
        kernel,
        out_shape=outs,
        grid=(1,),
        in_specs=specs,
        out_specs=[VMEM] * len(outs),
        scratch_shapes=scratch,
        cost_estimate=cost,
        compiler_params=pltpu.CompilerParams(vmem_limit_bytes=mib * 2**20),
    )


def bit(name):
    return 1 << (len(BITS) - 1 - BITS.index(name))


def members(order):
    rest = [bit(name) for name in BITS if name not in order]
    bases = [sum(w for k, w in enumerate(rest) if i >> k & 1) for i in range(1 << len(rest))]
    weight = [bit(name) for name in reversed(order)]
    places = [sum(w for k, w in enumerate(weight) if i >> k & 1) for i in range(1 << len(order))]
    return [[base + place for place in places] for base in bases]


def exchange(x, order):
    rows = x.shape[0]
    x = x.reshape(1 << len(order), 1, (rows * LANES) >> len(order))
    return lax.all_to_all(x, "d", 0, 0, tiled=True, axis_index_groups=members(order)).reshape(rows, LANES)


def partner(x, name):
    return lax.ppermute(x, "d", [(i, i ^ bit(name)) for i in range(1 << len(BITS))])


def local(signals, leaf_maps, root_maps, translations, source_list, type_list):
    blocks, rank, width = leaf_maps.shape
    waves = signals.shape[0]
    levels, kinds = translations.shape[:2]
    sources, types = jnp.swapaxes(source_list, 1, 2), jnp.swapaxes(type_list, 1, 2)
    root_maps = jnp.swapaxes(root_maps, 1, 2)
    held = pltpu.VMEM((blocks, waves, LANES), BF16)
    flat = jax.ShapeDtypeStruct((waves * blocks // 2, LANES), F32)
    mine = (lax.axis_index("d") & bit(FOLDED)).reshape(1)
    (x,) = call(
        start_kernel,
        [jax.ShapeDtypeStruct((waves * blocks, LANES), F32)],
        [SMEM, SMEM, SMEM, HBM, HBM, HBM],
        [
            held,
            pltpu.VMEM((kinds, 2 * rank, LANES), BF16),
            pltpu.VMEM((kinds, rank, rank), F32),
            pltpu.VMEM((waves, blocks * width), F32),
            pltpu.VMEM((blocks, rank, width), F32),
            pltpu.SemaphoreType.DMA((3, 3)),
        ],
        mib=60,
    )(sources, types, mine, translations, signals, leaf_maps)
    weights, root_weights = call(
        prepare_kernel,
        [
            jax.ShapeDtypeStruct((levels - 1, kinds, 2 * rank, LANES), BF16),
            jax.ShapeDtypeStruct((blocks, 4 * rank, width), BF16),
        ],
        [VMEM, VMEM],
        cost=pl.CostEstimate(flops=2**24, bytes_accessed=2**23, transcendentals=0),
    )(translations, root_maps)
    x = exchange(x, (FOLDED,) + GROUP)
    own, other = call(middle_kernel, [flat, flat], [SMEM, SMEM, VMEM, VMEM], [held, held])(sources, types, weights, x)
    (x,) = call(end_kernel, [flat], [SMEM, SMEM, VMEM, VMEM, VMEM], [held, held])(
        sources, types, weights, own, partner(other, "c")
    )
    (out,) = call(root_kernel, [jax.ShapeDtypeStruct((waves, blocks * width), F32)], [VMEM, VMEM])(
        exchange(x, GROUP), root_weights
    )
    return out


def solution(mesh):
    line = Mesh(mesh.devices.reshape(-1), ("d",))
    placed = (P(None, "d"), P("d", None, None), P("d", None, None), P(), P(), P())
    return jax.shard_map(local, mesh=line, in_specs=placed, out_specs=P(None, "d"), check_vma=False)
```

```python
import functools

import jax
import jax.numpy as jnp
from jax import lax
from jax.experimental import pallas as pl
from jax.experimental.pallas import tpu as pltpu
from jax.sharding import Mesh, PartitionSpec as P

BITS = ("z1", "z0", "y1", "y0", "x1", "x0", "zh", "c")
GROUP = ("z1", "z0", "y1", "x1", "x0", "zh")
FOLDED = "y0"
FLIPS = ("y0", "y1", "z0", "z1", "c", "zh", "x0", "x1")
LANES = 128
F32, BF16 = jnp.float32, jnp.bfloat16
NT = (((1,), (1,)), ((), ()))


def row_mask(level):
    return 1 << (len(GROUP) - 1 - GROUP.index(FLIPS[level]))


def dot_nt(a, b):
    return lax.dot_general(a, b, NT, preferred_element_type=F32)


def split(x):
    hi = x.astype(BF16)
    return hi, (x - hi.astype(F32)).astype(BF16)


def low_lanes(shape):
    return lax.broadcasted_iota(jnp.int32, shape, 1) < LANES // 2


def turn(x):
    return pltpu.roll(x, LANES // 2, 1)


def hi_lo_lanes(x):
    hi = x.astype(BF16).astype(F32)
    return jnp.where(low_lanes(x.shape), hi, x - hi).astype(BF16)


def flip_rows(v, mask):
    groups = [v[8 * i : 8 * i + 8] for i in range(v.shape[0] // 8)]
    if mask >= 8:
        groups = [groups[i ^ (mask // 8)] for i in range(len(groups))]
    elif mask == 4:
        groups = [pltpu.roll(g, 4, 0) for g in groups]
    else:
        bit = (lax.broadcasted_iota(jnp.int32, (8, LANES), 0) & mask) != 0
        groups = [jnp.where(bit, pltpu.roll(g, mask, 0), pltpu.roll(g, 8 - mask, 0)) for g in groups]
    return jnp.concatenate(groups, axis=0)


def pair_rows(ref, pair, first=0):
    return pl.ds(first * 12 + pair, 64, stride=12)


def put_pair(held, pair, x):
    turned = turn(x)
    low = low_lanes(x.shape)
    held[2 * pair] = hi_lo_lanes(jnp.where(low, x, turned))
    held[2 * pair + 1] = hi_lo_lanes(jnp.where(low, turned, x))


def put_weights(mat, out_ref):
    hi, lo = split(mat.T)
    both = jnp.concatenate([hi, lo], axis=1)
    rank = mat.shape[0]
    out_ref[:rank] = both
    out_ref[rank:] = both


def two_terms(level, block, entry, sources, types, back, held, weights):
    left = [held[sources[level, entry + i, block] - back] for i in range(2)]
    right = [weights[types[level, entry + i, block]] for i in range(2)]
    return jnp.dot(jnp.concatenate(left, axis=1), jnp.concatenate(right, axis=0), preferred_element_type=F32)


def level_step(level, sources, types, held, weights, emit):
    blocks = held.shape[0]

    def pair_step(pair, carry):
        terms = []
        for block in (2 * pair, 2 * pair + 1):
            terms.append(two_terms(level, block, 0, sources, types, 0, held, weights))
            terms.append(two_terms(level, block, 2, sources, types, blocks, held, weights))
        emit(pair, *terms)
        return carry

    lax.fori_loop(0, blocks // 2, pair_step, 0, unroll=6)


def flip_and_keep(held, mask):
    def emit(pair, own_even, other_even, own_odd, other_odd):
        for block, own, other in ((2 * pair, own_even, other_even), (2 * pair + 1, own_odd, other_odd)):
            total = own + flip_rows(other, mask)
            held[block] = hi_lo_lanes(total + turn(total))

    return emit


def flip_and_give(out_ref, mask):
    def emit(pair, own_even, other_even, own_odd, other_odd):
        even = own_even + flip_rows(other_even, mask)
        odd = own_odd + flip_rows(other_odd, mask)
        out_ref[pair_rows(out_ref, pair), :] = join(even, odd)

    return emit


def join(even, odd):
    low = low_lanes(even.shape)
    return jnp.where(low, even, odd) + turn(jnp.where(low, odd, even))


def give_both(own_ref, other_ref):
    def emit(pair, own_even, other_even, own_odd, other_odd):
        own_ref[pair_rows(own_ref, pair), :] = join(own_even, own_odd)
        other_ref[pair_rows(other_ref, pair), :] = join(other_even, other_odd)

    return emit


def give_by_bit(mine, out_ref):
    def emit(pair, own_even, other_even, own_odd, other_odd):
        own, other = join(own_even, own_odd), join(other_even, other_odd)
        out_ref[pair_rows(out_ref, pair), :] = jnp.where(mine == 0, own, other)
        out_ref[pair_rows(out_ref, pair, 64), :] = jnp.where(mine == 0, other, own)

    return emit


def run_levels(first, count, sources, types, held, weights, last):
    for i in range(count):
        now, then = held[i % 2], held[(i + 1) % 2]
        emit = last if i == count - 1 else flip_and_keep(then, row_mask(first + i))
        level_step(first + i, sources, types, now, weights.at[i], emit)


def start_kernel(
    sources, types, mine, tables, signals, maps, out_ref, early, held, weights, table_in, signals_in, maps_in, sems, table_sems
):
    blocks, rank, width = maps.shape
    parts = sems.shape[1]
    some = blocks // parts
    table_copies = []
    for level in range(table_in.shape[0]):
        table_copies.append(pltpu.make_async_copy(tables.at[level], table_in.at[level], table_sems.at[level]))
        table_copies[-1].start()
    copies = []
    for i in range(parts):
        lanes, rows = pl.ds(i * some * width, some * width), pl.ds(i * some, some)
        copies.append(
            (
                pltpu.make_async_copy(signals.at[:, lanes], signals_in.at[:, lanes], sems.at[0, i]),
                pltpu.make_async_copy(maps.at[rows], maps_in.at[rows], sems.at[1, i]),
            )
        )
        for copy in copies[-1]:
            copy.start()
    for level, copy in enumerate(table_copies):
        copy.wait()
        for kind in range(weights.shape[0]):
            put_weights(table_in[level, kind], weights.at[kind] if level == 0 else early.at[level - 1, kind])

    def leaf(k, carry):
        wave_hi, wave_lo = split(signals_in[:, pl.ds(pl.multiple_of(k * width, width), width)])
        map_hi, map_lo = split(maps_in[k])
        left = jnp.concatenate([wave_hi, wave_lo], axis=1)
        both = jnp.concatenate([map_hi, map_lo], axis=0)
        total = dot_nt(left, jnp.concatenate([both, both], axis=1))
        held[k] = hi_lo_lanes(total + turn(total))
        return carry

    for i in range(parts):
        for copy in copies[i]:
            copy.wait()
        lax.fori_loop(i * some, (i + 1) * some, leaf, 0, unroll=some)
    level_step(0, sources, types, held, weights, give_by_bit(mine[0], out_ref))


def prepare_tables(tables, weights):
    def table(level, carry):
        for kind in range(tables.shape[1]):
            put_weights(tables[level, kind], weights.at[level, kind])
        return carry

    lax.fori_loop(0, tables.shape[0], table, 0)


def prepare_late(tables, maps, weights, root_weights):
    prepare_tables(tables.at[5:], weights)

    def root(block, carry):
        hi, lo = split(maps[block])
        root_weights[block] = jnp.concatenate([hi, hi, lo, lo], axis=0)
        return carry

    lax.fori_loop(0, maps.shape[0], root, 0, unroll=4)


def middle_kernel(sources, types, weights, x_ref, own_ref, other_ref, held, held_too):
    for pair in range(held.shape[0] // 2):
        put_pair(held, pair, x_ref[pair_rows(x_ref, pair), :] + x_ref[pair_rows(x_ref, pair, 64), :])
    run_levels(1, 4, sources, types, (held, held_too), weights, give_both(own_ref, other_ref))


def end_kernel(sources, types, weights, own_ref, other_ref, out_ref, held, held_too):
    for pair in range(held.shape[0] // 2):
        rows = pair_rows(own_ref, pair)
        put_pair(held, pair, own_ref[rows, :] + other_ref[rows, :])
    run_levels(5, 3, sources, types, (held, held_too), weights, flip_and_give(out_ref, row_mask(7)))


def root_kernel(x_ref, weights, out_ref):
    blocks, width = weights.shape[0], weights.shape[2]

    def body(pair, carry):
        x = x_ref[pair_rows(x_ref, pair), :]
        turned = turn(x)
        low = low_lanes(x.shape)
        for block, value in ((2 * pair, jnp.where(low, x, turned)), (2 * pair + 1, jnp.where(low, turned, x))):
            left = hi_lo_lanes(value)
            out = jnp.dot(jnp.concatenate([left, left], axis=1), weights[block], preferred_element_type=F32)
            out_ref[:, pl.ds(pl.multiple_of(block * width, width), width)] = out
        return carry

    lax.fori_loop(0, blocks // 2, body, 0, unroll=4)


VMEM = pl.BlockSpec(memory_space=pltpu.VMEM)
SMEM = pl.BlockSpec(memory_space=pltpu.SMEM)
HBM = pl.BlockSpec(memory_space=pltpu.HBM)


def call(kernel, outs, specs, scratch=(), mib=12, cost=None):
    return pl.pallas_call(
        kernel,
        out_shape=outs,
        grid=(1,),
        in_specs=specs,
        out_specs=[VMEM] * len(outs),
        scratch_shapes=scratch,
        cost_estimate=cost,
        compiler_params=pltpu.CompilerParams(vmem_limit_bytes=mib * 2**20),
    )


def bit(name):
    return 1 << (len(BITS) - 1 - BITS.index(name))


def members(order):
    rest = [bit(name) for name in BITS if name not in order]
    bases = [sum(w for k, w in enumerate(rest) if i >> k & 1) for i in range(1 << len(rest))]
    weight = [bit(name) for name in reversed(order)]
    places = [sum(w for k, w in enumerate(weight) if i >> k & 1) for i in range(1 << len(order))]
    return [[base + place for place in places] for base in bases]


def exchange(x, order):
    rows = x.shape[0]
    x = x.reshape(1 << len(order), 1, (rows * LANES) >> len(order))
    return lax.all_to_all(x, "d", 0, 0, tiled=True, axis_index_groups=members(order)).reshape(rows, LANES)


def partner(x, name):
    return lax.ppermute(x, "d", [(i, i ^ bit(name)) for i in range(1 << len(BITS))])


def local(signals, leaf_maps, root_maps, translations, source_list, type_list):
    blocks, rank, width = leaf_maps.shape
    waves = signals.shape[0]
    levels, kinds = translations.shape[:2]
    sources, types = jnp.swapaxes(source_list, 1, 2), jnp.swapaxes(type_list, 1, 2)
    root_maps = jnp.swapaxes(root_maps, 1, 2)
    held = pltpu.VMEM((blocks, waves, LANES), BF16)
    flat = jax.ShapeDtypeStruct((waves * blocks // 2, LANES), F32)
    mine = (lax.axis_index("d") & bit(FOLDED)).reshape(1)
    def prepared(count):
        return jax.ShapeDtypeStruct((count, kinds, 2 * rank, LANES), BF16)

    x, early = call(
        start_kernel,
        [jax.ShapeDtypeStruct((waves * blocks, LANES), F32), prepared(4)],
        [SMEM, SMEM, SMEM, HBM, HBM, HBM],
        [
            held,
            pltpu.VMEM((kinds, 2 * rank, LANES), BF16),
            pltpu.VMEM((5, kinds, rank, rank), F32),
            pltpu.VMEM((waves, blocks * width), F32),
            pltpu.VMEM((blocks, rank, width), F32),
            pltpu.SemaphoreType.DMA((2, 3)),
            pltpu.SemaphoreType.DMA((5,)),
        ],
        mib=60,
    )(sources, types, mine, translations, signals, leaf_maps)
    x = exchange(x, (FOLDED,) + GROUP)
    own, other = call(middle_kernel, [flat, flat], [SMEM, SMEM, VMEM, VMEM], [held, held])(sources, types, early, x)
    other, translations, root_maps = lax.optimization_barrier((other, translations, root_maps))
    received = partner(other, "c")
    late, root_weights = call(
        prepare_late,
        [prepared(3), jax.ShapeDtypeStruct((blocks, 4 * rank, width), BF16)],
        [VMEM, VMEM],
        cost=pl.CostEstimate(flops=2**24, bytes_accessed=2**22, transcendentals=0),
    )(translations, root_maps)
    (x,) = call(end_kernel, [flat], [SMEM, SMEM, VMEM, VMEM, VMEM], [held, held])(sources, types, late, own, received)
    (out,) = call(root_kernel, [jax.ShapeDtypeStruct((waves, blocks * width), F32)], [VMEM, VMEM])(
        exchange(x, GROUP), root_weights
    )
    return out


def solution(mesh):
    line = Mesh(mesh.devices.reshape(-1), ("d",))
    placed = (P(None, "d"), P("d", None, None), P("d", None, None), P(), P(), P())
    return jax.shard_map(local, mesh=line, in_specs=placed, out_specs=P(None, "d"), check_vma=False)
```

```python
import functools

import jax
import jax.numpy as jnp
from jax import lax
from jax.experimental import pallas as pl
from jax.experimental.pallas import tpu as pltpu
from jax.sharding import Mesh, PartitionSpec as P

BITS = ("z1", "z0", "y1", "y0", "x1", "x0", "zh", "c")
GROUP = ("z1", "z0", "y1", "x1", "x0", "zh")
FOLDED = "y0"
FLIPS = ("y0", "y1", "z0", "z1", "c", "zh", "x0", "x1")
LANES = 128
F32, BF16 = jnp.float32, jnp.bfloat16
NT = (((1,), (1,)), ((), ()))


def row_mask(level):
    return 1 << (len(GROUP) - 1 - GROUP.index(FLIPS[level]))


def dot_nt(a, b):
    return lax.dot_general(a, b, NT, preferred_element_type=F32)


def split(x):
    hi = x.astype(BF16)
    return hi, (x - hi.astype(F32)).astype(BF16)


def low_lanes(shape):
    return lax.broadcasted_iota(jnp.int32, shape, 1) < LANES // 2


def turn(x):
    return pltpu.roll(x, LANES // 2, 1)


def hi_lo_lanes(x):
    hi = x.astype(BF16).astype(F32)
    return jnp.where(low_lanes(x.shape), hi, x - hi).astype(BF16)


def flip_rows(v, mask):
    groups = [v[8 * i : 8 * i + 8] for i in range(v.shape[0] // 8)]
    if mask >= 8:
        groups = [groups[i ^ (mask // 8)] for i in range(len(groups))]
    elif mask == 4:
        groups = [pltpu.roll(g, 4, 0) for g in groups]
    else:
        bit = (lax.broadcasted_iota(jnp.int32, (8, LANES), 0) & mask) != 0
        groups = [jnp.where(bit, pltpu.roll(g, mask, 0), pltpu.roll(g, 8 - mask, 0)) for g in groups]
    return jnp.concatenate(groups, axis=0)


def pair_rows(ref, pair, first=0):
    return pl.ds(first * 12 + pair, 64, stride=12)


def put_pair(held, pair, x):
    turned = turn(x)
    low = low_lanes(x.shape)
    held[2 * pair] = hi_lo_lanes(jnp.where(low, x, turned))
    held[2 * pair + 1] = hi_lo_lanes(jnp.where(low, turned, x))


def put_weights(mat, out_ref):
    hi, lo = split(mat.T)
    both = jnp.concatenate([hi, lo], axis=1)
    rank = mat.shape[0]
    out_ref[:rank] = both
    out_ref[rank:] = both


def two_terms(level, block, entry, sources, types, back, held, weights):
    left = [held[sources[level, entry + i, block] - back] for i in range(2)]
    right = [weights[types[level, entry + i, block]] for i in range(2)]
    return jnp.dot(jnp.concatenate(left, axis=1), jnp.concatenate(right, axis=0), preferred_element_type=F32)


def level_step(level, sources, types, held, weights, emit):
    blocks = held.shape[0]

    def pair_step(pair, carry):
        terms = []
        for block in (2 * pair, 2 * pair + 1):
            terms.append(two_terms(level, block, 0, sources, types, 0, held, weights))
            terms.append(two_terms(level, block, 2, sources, types, blocks, held, weights))
        emit(pair, *terms)
        return carry

    lax.fori_loop(0, blocks // 2, pair_step, 0, unroll=6)


def flip_and_keep(held, mask):
    def emit(pair, own_even, other_even, own_odd, other_odd):
        for block, own, other in ((2 * pair, own_even, other_even), (2 * pair + 1, own_odd, other_odd)):
            total = own + flip_rows(other, mask)
            held[block] = hi_lo_lanes(total + turn(total))

    return emit


def flip_and_give(out_ref, mask):
    def emit(pair, own_even, other_even, own_odd, other_odd):
        even = own_even + flip_rows(other_even, mask)
        odd = own_odd + flip_rows(other_odd, mask)
        out_ref[pair_rows(out_ref, pair), :] = join(even, odd)

    return emit


def join(even, odd):
    low = low_lanes(even.shape)
    return jnp.where(low, even, odd) + turn(jnp.where(low, odd, even))


def give_both(own_ref, other_ref):
    def emit(pair, own_even, other_even, own_odd, other_odd):
        own_ref[pair_rows(own_ref, pair), :] = join(own_even, own_odd)
        other_ref[pair_rows(other_ref, pair), :] = join(other_even, other_odd)

    return emit


def give_by_bit(mine, out_ref):
    def emit(pair, own_even, other_even, own_odd, other_odd):
        own, other = join(own_even, own_odd), join(other_even, other_odd)
        out_ref[pair_rows(out_ref, pair), :] = jnp.where(mine == 0, own, other)
        out_ref[pair_rows(out_ref, pair, 64), :] = jnp.where(mine == 0, other, own)

    return emit


def run_levels(first, count, sources, types, held, weights, last):
    for i in range(count):
        now, then = held[i % 2], held[(i + 1) % 2]
        emit = last if i == count - 1 else flip_and_keep(then, row_mask(first + i))
        level_step(first + i, sources, types, now, weights.at[i], emit)


def start_kernel(
    sources, types, mine, tables, signals, maps, out_ref, early, held, weights, table_in, signals_in, maps_in, sems, table_sems
):
    blocks, rank, width = maps.shape
    parts = sems.shape[1]
    some = blocks // parts
    table_copies = []
    for level in range(table_in.shape[0]):
        table_copies.append(pltpu.make_async_copy(tables.at[level], table_in.at[level], table_sems.at[level]))
        table_copies[-1].start()
    copies = []
    for i in range(parts):
        lanes, rows = pl.ds(i * some * width, some * width), pl.ds(i * some, some)
        copies.append(
            (
                pltpu.make_async_copy(signals.at[:, lanes], signals_in.at[:, lanes], sems.at[0, i]),
                pltpu.make_async_copy(maps.at[rows], maps_in.at[rows], sems.at[1, i]),
            )
        )
        for copy in copies[-1]:
            copy.start()
    for level, copy in enumerate(table_copies):
        copy.wait()
        for kind in range(weights.shape[0]):
            put_weights(table_in[level, kind], weights.at[kind] if level == 0 else early.at[level - 1, kind])

    def leaf(k, carry):
        wave_hi, wave_lo = split(signals_in[:, pl.ds(pl.multiple_of(k * width, width), width)])
        map_hi, map_lo = split(maps_in[k])
        left = jnp.concatenate([wave_hi, wave_lo], axis=1)
        both = jnp.concatenate([map_hi, map_lo], axis=0)
        total = dot_nt(left, jnp.concatenate([both, both], axis=1))
        held[k] = hi_lo_lanes(total + turn(total))
        return carry

    for i in range(parts):
        for copy in copies[i]:
            copy.wait()
        lax.fori_loop(i * some, (i + 1) * some, leaf, 0, unroll=some)
    level_step(0, sources, types, held, weights, give_by_bit(mine[0], out_ref))


def prepare_tables(tables, weights):
    def table(level, carry):
        for kind in range(tables.shape[1]):
            put_weights(tables[level, kind], weights.at[level, kind])
        return carry

    lax.fori_loop(0, tables.shape[0], table, 0)


def prepare_late(tables, maps, weights, root_weights):
    prepare_tables(tables.at[5:], weights)

    def root(block, carry):
        hi, lo = split(maps[block])
        root_weights[block] = jnp.concatenate([hi, hi, lo, lo], axis=0)
        return carry

    lax.fori_loop(0, maps.shape[0], root, 0, unroll=4)


def middle_kernel(sources, types, weights, x_ref, own_ref, other_ref, held, held_too):
    for pair in range(held.shape[0] // 2):
        put_pair(held, pair, x_ref[pair_rows(x_ref, pair), :] + x_ref[pair_rows(x_ref, pair, 64), :])
    run_levels(1, 4, sources, types, (held, held_too), weights, give_both(own_ref, other_ref))


def end_kernel(sources, types, weights, own_ref, other_ref, out_ref, held, held_too):
    for pair in range(held.shape[0] // 2):
        rows = pair_rows(own_ref, pair)
        put_pair(held, pair, own_ref[rows, :] + other_ref[rows, :])
    run_levels(5, 3, sources, types, (held, held_too), weights, flip_and_give(out_ref, row_mask(7)))


def root_kernel(x_ref, weights, out_ref):
    blocks, width = weights.shape[0], weights.shape[2]

    def body(pair, carry):
        x = x_ref[pair_rows(x_ref, pair), :]
        turned = turn(x)
        low = low_lanes(x.shape)
        for block, value in ((2 * pair, jnp.where(low, x, turned)), (2 * pair + 1, jnp.where(low, turned, x))):
            left = hi_lo_lanes(value)
            out = jnp.dot(jnp.concatenate([left, left], axis=1), weights[block], preferred_element_type=F32)
            out_ref[:, pl.ds(pl.multiple_of(block * width, width), width)] = out
        return carry

    lax.fori_loop(0, blocks // 2, body, 0, unroll=4)


VMEM = pl.BlockSpec(memory_space=pltpu.VMEM)
SMEM = pl.BlockSpec(memory_space=pltpu.SMEM)
HBM = pl.BlockSpec(memory_space=pltpu.HBM)


def call(kernel, outs, specs, scratch=(), mib=12, cost=None):
    return pl.pallas_call(
        kernel,
        out_shape=outs,
        grid=(1,),
        in_specs=specs,
        out_specs=[VMEM] * len(outs),
        scratch_shapes=scratch,
        cost_estimate=cost,
        compiler_params=pltpu.CompilerParams(vmem_limit_bytes=int(mib * 2**20)),
    )


def bit(name):
    return 1 << (len(BITS) - 1 - BITS.index(name))


def members(order):
    rest = [bit(name) for name in BITS if name not in order]
    bases = [sum(w for k, w in enumerate(rest) if i >> k & 1) for i in range(1 << len(rest))]
    weight = [bit(name) for name in reversed(order)]
    places = [sum(w for k, w in enumerate(weight) if i >> k & 1) for i in range(1 << len(order))]
    return [[base + place for place in places] for base in bases]


def exchange(x, order):
    rows = x.shape[0]
    x = x.reshape(1 << len(order), 1, (rows * LANES) >> len(order))
    return lax.all_to_all(x, "d", 0, 0, tiled=True, axis_index_groups=members(order)).reshape(rows, LANES)


def partner(x, name):
    return lax.ppermute(x, "d", [(i, i ^ bit(name)) for i in range(1 << len(BITS))])


def local(signals, leaf_maps, root_maps, translations, source_list, type_list):
    blocks, rank, width = leaf_maps.shape
    waves = signals.shape[0]
    levels, kinds = translations.shape[:2]
    sources, types = jnp.swapaxes(source_list, 1, 2), jnp.swapaxes(type_list, 1, 2)
    root_maps = jnp.swapaxes(root_maps, 1, 2)
    held = pltpu.VMEM((blocks, waves, LANES), BF16)
    flat = jax.ShapeDtypeStruct((waves * blocks // 2, LANES), F32)
    mine = (lax.axis_index("d") & bit(FOLDED)).reshape(1)
    def prepared(count):
        return jax.ShapeDtypeStruct((count, kinds, 2 * rank, LANES), BF16)

    x, early = call(
        start_kernel,
        [jax.ShapeDtypeStruct((waves * blocks, LANES), F32), prepared(4)],
        [SMEM, SMEM, SMEM, HBM, HBM, HBM],
        [
            held,
            pltpu.VMEM((kinds, 2 * rank, LANES), BF16),
            pltpu.VMEM((5, kinds, rank, rank), F32),
            pltpu.VMEM((waves, blocks * width), F32),
            pltpu.VMEM((blocks, rank, width), F32),
            pltpu.SemaphoreType.DMA((2, 3)),
            pltpu.SemaphoreType.DMA((5,)),
        ],
        mib=53,
    )(sources, types, mine, translations, signals, leaf_maps)
    x = exchange(x, (FOLDED,) + GROUP)
    own, other = call(middle_kernel, [flat, flat], [SMEM, SMEM, VMEM, VMEM], [held, held])(sources, types, early, x)
    other, translations, root_maps = lax.optimization_barrier((other, translations, root_maps))
    received = partner(other, "c")
    late, root_weights = call(
        prepare_late,
        [prepared(3), jax.ShapeDtypeStruct((blocks, 4 * rank, width), BF16)],
        [VMEM, VMEM],
        cost=pl.CostEstimate(flops=2**24, bytes_accessed=2**22, transcendentals=0),
    )(translations, root_maps)
    (x,) = call(end_kernel, [flat], [SMEM, SMEM, VMEM, VMEM, VMEM], [held, held])(sources, types, late, own, received)
    (out,) = call(root_kernel, [jax.ShapeDtypeStruct((waves, blocks * width), F32)], [VMEM, VMEM])(
        exchange(x, GROUP), root_weights
    )
    return out


def solution(mesh):
    line = Mesh(mesh.devices.reshape(-1), ("d",))
    placed = (P(None, "d"), P("d", None, None), P("d", None, None), P(), P(), P())
    return jax.shard_map(local, mesh=line, in_specs=placed, out_specs=P(None, "d"), check_vma=False)
```

```python
import functools

import jax
import jax.numpy as jnp
from jax import lax
from jax.experimental import pallas as pl
from jax.experimental.pallas import tpu as pltpu
from jax.sharding import Mesh, PartitionSpec as P

BITS = ("z1", "z0", "y1", "y0", "x1", "x0", "zh", "c")
GROUP = ("z1", "z0", "y1", "x1", "x0", "zh")
FLIPS = ("y0", "y1", "z0", "z1", "c", "zh", "x0", "x1")
LANES = 128
F32, BF16 = jnp.float32, jnp.bfloat16
NT = (((1,), (1,)), ((), ()))


def row_mask(level):
    return 1 << (len(GROUP) - 1 - GROUP.index(FLIPS[level]))


def dot_nt(a, b):
    return lax.dot_general(a, b, NT, preferred_element_type=F32)


def split(x):
    hi = x.astype(BF16)
    return hi, (x - hi.astype(F32)).astype(BF16)


def low_lanes(shape):
    return lax.broadcasted_iota(jnp.int32, shape, 1) < LANES // 2


def turn(x):
    return pltpu.roll(x, LANES // 2, 1)


def hi_lo_lanes(x):
    hi = x.astype(BF16).astype(F32)
    return jnp.where(low_lanes(x.shape), hi, x - hi).astype(BF16)


def flip_rows(v, mask):
    groups = [v[8 * i : 8 * i + 8] for i in range(v.shape[0] // 8)]
    if mask >= 8:
        groups = [groups[i ^ (mask // 8)] for i in range(len(groups))]
    elif mask == 4:
        groups = [pltpu.roll(g, 4, 0) for g in groups]
    else:
        bit = (lax.broadcasted_iota(jnp.int32, (8, LANES), 0) & mask) != 0
        groups = [jnp.where(bit, pltpu.roll(g, mask, 0), pltpu.roll(g, 8 - mask, 0)) for g in groups]
    return jnp.concatenate(groups, axis=0)


def pair_rows(ref, pair):
    return pl.ds(pair, ref.shape[0] // 12, stride=12)


def put_pair(held, pair, x):
    turned = turn(x)
    low = low_lanes(x.shape)
    held[2 * pair] = hi_lo_lanes(jnp.where(low, x, turned))
    held[2 * pair + 1] = hi_lo_lanes(jnp.where(low, turned, x))


def put_weights(mat, out_ref):
    hi, lo = split(mat.T)
    both = jnp.concatenate([hi, lo], axis=1)
    rank = mat.shape[0]
    out_ref[:rank] = both
    out_ref[rank:] = both


def two_terms(level, block, entry, sources, types, back, held, weights):
    left = [held[sources[level, entry + i, block] - back] for i in range(2)]
    right = [weights[types[level, entry + i, block]] for i in range(2)]
    return jnp.dot(jnp.concatenate(left, axis=1), jnp.concatenate(right, axis=0), preferred_element_type=F32)


def level_step(level, sources, types, held, weights, emit):
    blocks = held.shape[0]

    def pair_step(pair, carry):
        terms = []
        for block in (2 * pair, 2 * pair + 1):
            terms.append(two_terms(level, block, 0, sources, types, 0, held, weights))
            terms.append(two_terms(level, block, 2, sources, types, blocks, held, weights))
        emit(pair, *terms)
        return carry

    lax.fori_loop(0, blocks // 2, pair_step, 0, unroll=True)


def half_level(level, entry, back, sources, types, held, weights, out_ref):
    def pair_step(pair, carry):
        even = two_terms(level, 2 * pair, entry, sources, types, back, held, weights)
        odd = two_terms(level, 2 * pair + 1, entry, sources, types, back, held, weights)
        out_ref[pair_rows(out_ref, pair), :] = join(even, odd)
        return carry

    lax.fori_loop(0, held.shape[0] // 2, pair_step, 0, unroll=True)


def flip_and_keep(held, mask):
    def emit(pair, own_even, other_even, own_odd, other_odd):
        for block, own, other in ((2 * pair, own_even, other_even), (2 * pair + 1, own_odd, other_odd)):
            total = own + flip_rows(other, mask)
            held[block] = hi_lo_lanes(total + turn(total))

    return emit


def flip_and_give(out_ref, mask):
    def emit(pair, own_even, other_even, own_odd, other_odd):
        even = own_even + flip_rows(other_even, mask)
        odd = own_odd + flip_rows(other_odd, mask)
        out_ref[pair_rows(out_ref, pair), :] = join(even, odd)

    return emit


def join(even, odd):
    low = low_lanes(even.shape)
    return jnp.where(low, even, odd) + turn(jnp.where(low, odd, even))


def give_both(own_ref, other_ref):
    def emit(pair, own_even, other_even, own_odd, other_odd):
        own_ref[pair_rows(own_ref, pair), :] = join(own_even, own_odd)
        other_ref[pair_rows(other_ref, pair), :] = join(other_even, other_odd)

    return emit


def run_levels(first, count, sources, types, held, weights, last):
    for i in range(count):
        now, then = held[i % 2], held[(i + 1) % 2]
        emit = last if i == count - 1 else flip_and_keep(then, row_mask(first + i))
        level_step(first + i, sources, types, now, weights.at[first + i - 1], emit)


def start_kernel(
    sources, types, tables, signals, maps, other_ref, held, weights, table_in, signals_in, maps_in, sems
):
    blocks, rank, width = maps.shape
    parts = sems.shape[1]
    some = blocks // parts
    table_copy = pltpu.make_async_copy(tables.at[0], table_in, sems.at[2, 0])
    table_copy.start()
    copies = []
    for i in range(parts):
        lanes, rows = pl.ds(i * some * width, some * width), pl.ds(i * some, some)
        copies.append(
            (
                pltpu.make_async_copy(signals.at[:, lanes], signals_in.at[:, lanes], sems.at[0, i]),
                pltpu.make_async_copy(maps.at[rows], maps_in.at[rows], sems.at[1, i]),
            )
        )
        for copy in copies[-1]:
            copy.start()
    table_copy.wait()
    for kind in range(weights.shape[0]):
        put_weights(table_in[kind], weights.at[kind])

    def leaf(k, carry):
        wave_hi, wave_lo = split(signals_in[:, pl.ds(pl.multiple_of(k * width, width), width)])
        map_hi, map_lo = split(maps_in[k])
        left = jnp.concatenate([wave_hi, wave_lo], axis=1)
        both = jnp.concatenate([map_hi, map_lo], axis=0)
        total = dot_nt(left, jnp.concatenate([both, both], axis=1))
        held[k] = hi_lo_lanes(total + turn(total))
        return carry

    for i in range(parts):
        for copy in copies[i]:
            copy.wait()
        lax.fori_loop(i * some, (i + 1) * some, leaf, 0, unroll=some)
    half_level(0, 2, blocks, sources, types, held, weights, other_ref)


def prepare_kernel(sources, types, tables, maps, held, own_ref, weights, root_weights, weights_here):
    for kind in range(tables.shape[1]):
        put_weights(tables[0, kind], weights_here.at[kind])
    half_level(0, 0, 0, sources, types, held, weights_here, own_ref)

    def table(level, carry):
        for kind in range(tables.shape[1]):
            put_weights(tables[level + 1, kind], weights.at[level, kind])
        return carry

    lax.fori_loop(0, tables.shape[0] - 1, table, 0)

    def root(block, carry):
        hi, lo = split(maps[block])
        root_weights[block] = jnp.concatenate([hi, hi, lo, lo], axis=0)
        return carry

    lax.fori_loop(0, maps.shape[0], root, 0, unroll=4)


def middle_kernel(sources, types, weights, x_ref, own_ref, other_ref, held, held_too):
    for pair in range(held.shape[0] // 2):
        put_pair(held, pair, x_ref[pair_rows(x_ref, pair), :])
    run_levels(1, 4, sources, types, (held, held_too), weights, give_both(own_ref, other_ref))


def end_kernel(sources, types, weights, own_ref, other_ref, out_ref, held, held_too):
    for pair in range(held.shape[0] // 2):
        rows = pair_rows(own_ref, pair)
        put_pair(held, pair, own_ref[rows, :] + other_ref[rows, :])
    run_levels(5, 3, sources, types, (held, held_too), weights, flip_and_give(out_ref, row_mask(7)))


def root_kernel(x_ref, weights, out_ref):
    blocks, width = weights.shape[0], weights.shape[2]

    def body(pair, carry):
        x = x_ref[pair_rows(x_ref, pair), :]
        turned = turn(x)
        low = low_lanes(x.shape)
        for block, value in ((2 * pair, jnp.where(low, x, turned)), (2 * pair + 1, jnp.where(low, turned, x))):
            left = hi_lo_lanes(value)
            out = jnp.dot(jnp.concatenate([left, left], axis=1), weights[block], preferred_element_type=F32)
            out_ref[:, pl.ds(pl.multiple_of(block * width, width), width)] = out
        return carry

    lax.fori_loop(0, blocks // 2, body, 0, unroll=4)


VMEM = pl.BlockSpec(memory_space=pltpu.VMEM)
SMEM = pl.BlockSpec(memory_space=pltpu.SMEM)
HBM = pl.BlockSpec(memory_space=pltpu.HBM)


def call(kernel, outs, specs, scratch=(), mib=12, cost=None):
    return pl.pallas_call(
        kernel,
        out_shape=outs,
        grid=(1,),
        in_specs=specs,
        out_specs=[VMEM] * len(outs),
        scratch_shapes=scratch,
        cost_estimate=cost,
        compiler_params=pltpu.CompilerParams(vmem_limit_bytes=mib * 2**20),
    )


def exchange(x):
    rows = x.shape[0]
    x = x.reshape(64, 1, rows * LANES // 64)
    return lax.all_to_all(x, GROUP, 0, 0, tiled=True).reshape(rows, LANES)


def partner(x, axis):
    return lax.ppermute(x, axis, [(0, 1), (1, 0)])


def local(signals, leaf_maps, root_maps, translations, source_list, type_list):
    blocks, rank, width = leaf_maps.shape
    waves = signals.shape[0]
    levels, kinds = translations.shape[:2]
    sources, types = jnp.swapaxes(source_list, 1, 2), jnp.swapaxes(type_list, 1, 2)
    root_maps = jnp.swapaxes(root_maps, 1, 2)
    held = pltpu.VMEM((blocks, waves, LANES), BF16)
    flat = jax.ShapeDtypeStruct((waves * blocks // 2, LANES), F32)
    other, left = call(
        start_kernel,
        [flat, jax.ShapeDtypeStruct((blocks, waves, LANES), BF16)],
        [SMEM, SMEM, HBM, HBM, HBM],
        [
            pltpu.VMEM((kinds, 2 * rank, LANES), BF16),
            pltpu.VMEM((kinds, rank, rank), F32),
            pltpu.VMEM((waves, blocks * width), F32),
            pltpu.VMEM((blocks, rank, width), F32),
            pltpu.SemaphoreType.DMA((3, 3)),
        ],
        mib=60,
    )(sources, types, translations, signals, leaf_maps)
    received = partner(other, "y0")
    own, weights, root_weights = call(
        prepare_kernel,
        [
            flat,
            jax.ShapeDtypeStruct((levels - 1, kinds, 2 * rank, LANES), BF16),
            jax.ShapeDtypeStruct((blocks, 4 * rank, width), BF16),
        ],
        [SMEM, SMEM, VMEM, VMEM, VMEM],
        [pltpu.VMEM((kinds, 2 * rank, LANES), BF16)],
        cost=pl.CostEstimate(flops=2**24, bytes_accessed=2**23, transcendentals=0),
    )(sources, types, translations, root_maps, left)
    x, weights, root_weights = lax.optimization_barrier((own + received, weights, root_weights))
    x = exchange(x)
    own, other = call(middle_kernel, [flat, flat], [SMEM, SMEM, VMEM, VMEM], [held, held])(sources, types, weights, x)
    (x,) = call(end_kernel, [flat], [SMEM, SMEM, VMEM, VMEM, VMEM], [held, held])(
        sources, types, weights, own, partner(other, "c")
    )
    (out,) = call(root_kernel, [jax.ShapeDtypeStruct((waves, blocks * width), F32)], [VMEM, VMEM])(
        exchange(x), root_weights
    )
    return out


def solution(mesh):
    fine = Mesh(mesh.devices.reshape((2,) * len(BITS)), BITS)
    placed = (P(None, BITS), P(BITS, None, None), P(BITS, None, None), P(), P(), P())
    return jax.shard_map(local, mesh=fine, in_specs=placed, out_specs=P(None, BITS), check_vma=False)
```

```python
import functools

import jax
import jax.numpy as jnp
from jax import lax
from jax.experimental import pallas as pl
from jax.experimental.pallas import tpu as pltpu
from jax.sharding import Mesh, PartitionSpec as P

BITS = ("z1", "z0", "y1", "y0", "x1", "x0", "zh", "c")
GROUP = ("z1", "z0", "y1", "x1", "x0", "zh")
FLIPS = ("y0", "y1", "z0", "z1", "c", "zh", "x0", "x1")
LANES = 128
F32, BF16 = jnp.float32, jnp.bfloat16
NT = (((1,), (1,)), ((), ()))


def row_mask(level):
    return 1 << (len(GROUP) - 1 - GROUP.index(FLIPS[level]))


def dot_nt(a, b):
    return lax.dot_general(a, b, NT, preferred_element_type=F32)


def split(x):
    hi = x.astype(BF16)
    return hi, (x - hi.astype(F32)).astype(BF16)


def low_lanes(shape):
    return lax.broadcasted_iota(jnp.int32, shape, 1) < LANES // 2


def turn(x):
    return pltpu.roll(x, LANES // 2, 1)


def hi_lo_lanes(x):
    hi = x.astype(BF16).astype(F32)
    return jnp.where(low_lanes(x.shape), hi, x - hi).astype(BF16)


def flip_rows(v, mask):
    groups = [v[8 * i : 8 * i + 8] for i in range(v.shape[0] // 8)]
    if mask >= 8:
        groups = [groups[i ^ (mask // 8)] for i in range(len(groups))]
    elif mask == 4:
        groups = [pltpu.roll(g, 4, 0) for g in groups]
    else:
        bit = (lax.broadcasted_iota(jnp.int32, (8, LANES), 0) & mask) != 0
        groups = [jnp.where(bit, pltpu.roll(g, mask, 0), pltpu.roll(g, 8 - mask, 0)) for g in groups]
    return jnp.concatenate(groups, axis=0)


def pair_rows(ref, pair):
    return pl.ds(pair, ref.shape[0] // 12, stride=12)


def put_pair(held, pair, x):
    turned = turn(x)
    low = low_lanes(x.shape)
    held[2 * pair] = hi_lo_lanes(jnp.where(low, x, turned))
    held[2 * pair + 1] = hi_lo_lanes(jnp.where(low, turned, x))


def put_weights(mat, out_ref):
    hi, lo = split(mat.T)
    both = jnp.concatenate([hi, lo], axis=1)
    rank = mat.shape[0]
    out_ref[:rank] = both
    out_ref[rank:] = both


def two_terms(level, block, entry, sources, types, back, held, weights):
    left = [held[sources[level, entry + i, block] - back] for i in range(2)]
    right = [weights[types[level, entry + i, block]] for i in range(2)]
    return jnp.dot(jnp.concatenate(left, axis=1), jnp.concatenate(right, axis=0), preferred_element_type=F32)


def level_step(level, sources, types, held, weights, emit):
    blocks = held.shape[0]

    def pair_step(pair, carry):
        terms = []
        for block in (2 * pair, 2 * pair + 1):
            terms.append(two_terms(level, block, 0, sources, types, 0, held, weights))
            terms.append(two_terms(level, block, 2, sources, types, blocks, held, weights))
        emit(pair, *terms)
        return carry

    lax.fori_loop(0, blocks // 2, pair_step, 0, unroll=True)


def half_level(level, entry, back, sources, types, held, weights, out_ref):
    def pair_step(pair, carry):
        even = two_terms(level, 2 * pair, entry, sources, types, back, held, weights)
        odd = two_terms(level, 2 * pair + 1, entry, sources, types, back, held, weights)
        out_ref[pair_rows(out_ref, pair), :] = join(even, odd)
        return carry

    lax.fori_loop(0, held.shape[0] // 2, pair_step, 0, unroll=True)


def flip_and_keep(held, mask):
    def emit(pair, own_even, other_even, own_odd, other_odd):
        for block, own, other in ((2 * pair, own_even, other_even), (2 * pair + 1, own_odd, other_odd)):
            total = own + flip_rows(other, mask)
            held[block] = hi_lo_lanes(total + turn(total))

    return emit


def flip_and_give(out_ref, mask):
    def emit(pair, own_even, other_even, own_odd, other_odd):
        even = own_even + flip_rows(other_even, mask)
        odd = own_odd + flip_rows(other_odd, mask)
        out_ref[pair_rows(out_ref, pair), :] = join(even, odd)

    return emit


def join(even, odd):
    low = low_lanes(even.shape)
    return jnp.where(low, even, odd) + turn(jnp.where(low, odd, even))


def give_both(own_ref, other_ref):
    def emit(pair, own_even, other_even, own_odd, other_odd):
        own_ref[pair_rows(own_ref, pair), :] = join(own_even, own_odd)
        other_ref[pair_rows(other_ref, pair), :] = join(other_even, other_odd)

    return emit


def run_levels(first, count, sources, types, held, weights, last):
    for i in range(count):
        now, then = held[i % 2], held[(i + 1) % 2]
        emit = last if i == count - 1 else flip_and_keep(then, row_mask(first + i))
        level_step(first + i, sources, types, now, weights.at[i], emit)


def start_kernel(
    sources, types, tables, signals, maps, other_ref, left_ref, held, weights, table_in, signals_in, maps_in, sems
):
    blocks, rank, width = maps.shape
    parts = sems.shape[1]
    some = blocks // parts
    table_copy = pltpu.make_async_copy(tables.at[0], table_in, sems.at[2, 0])
    table_copy.start()
    copies = []
    for i in range(parts):
        lanes, rows = pl.ds(i * some * width, some * width), pl.ds(i * some, some)
        copies.append(
            (
                pltpu.make_async_copy(signals.at[:, lanes], signals_in.at[:, lanes], sems.at[0, i]),
                pltpu.make_async_copy(maps.at[rows], maps_in.at[rows], sems.at[1, i]),
            )
        )
        for copy in copies[-1]:
            copy.start()
    table_copy.wait()
    for kind in range(weights.shape[0]):
        put_weights(table_in[kind], weights.at[kind])

    def leaf(k, carry):
        wave_hi, wave_lo = split(signals_in[:, pl.ds(pl.multiple_of(k * width, width), width)])
        map_hi, map_lo = split(maps_in[k])
        left = jnp.concatenate([wave_hi, wave_lo], axis=1)
        both = jnp.concatenate([map_hi, map_lo], axis=0)
        total = dot_nt(left, jnp.concatenate([both, both], axis=1))
        held[k] = hi_lo_lanes(total + turn(total))
        return carry

    for i in range(parts):
        for copy in copies[i]:
            copy.wait()
        lax.fori_loop(i * some, (i + 1) * some, leaf, 0, unroll=some)
    left_copy = pltpu.make_async_copy(held, left_ref, sems.at[2, 1])
    left_copy.start()
    half_level(0, 2, blocks, sources, types, held, weights, other_ref)
    left_copy.wait()


def prepare_kernel(sources, types, tables, maps, held, own_ref, early, late, root_weights, weights_here):
    for kind in range(tables.shape[1]):
        put_weights(tables[0, kind], weights_here.at[kind])
    half_level(0, 0, 0, sources, types, held, weights_here, own_ref)

    for first, weights in ((1, early), (1 + early.shape[0], late)):

        def table(level, carry, first=first, weights=weights):
            for kind in range(tables.shape[1]):
                put_weights(tables[first + level, kind], weights.at[level, kind])
            return carry

        lax.fori_loop(0, weights.shape[0], table, 0)

    def root(block, carry):
        hi, lo = split(maps[block])
        root_weights[block] = jnp.concatenate([hi, hi, lo, lo], axis=0)
        return carry

    lax.fori_loop(0, maps.shape[0], root, 0, unroll=4)


def middle_kernel(sources, types, weights, x_ref, other_ref, left_ref, held, held_too):
    blocks = held.shape[0]
    for pair in range(blocks // 2):
        put_pair(held, pair, x_ref[pair_rows(x_ref, pair), :])
    run_levels(1, 3, sources, types, (held, held_too), weights, flip_and_keep(left_ref, row_mask(3)))
    half_level(4, 2, blocks, sources, types, left_ref, weights.at[3], other_ref)


def own_kernel(sources, types, weights, left, own_ref):
    half_level(4, 0, 0, sources, types, left, weights.at[0], own_ref)


def end_kernel(sources, types, weights, own_ref, other_ref, out_ref, held, held_too):
    for pair in range(held.shape[0] // 2):
        rows = pair_rows(own_ref, pair)
        put_pair(held, pair, own_ref[rows, :] + other_ref[rows, :])
    run_levels(5, 3, sources, types, (held, held_too), weights, flip_and_give(out_ref, row_mask(7)))


def root_kernel(x_ref, weights, out_ref):
    blocks, width = weights.shape[0], weights.shape[2]
    first = pl.program_id(0) * (blocks // 2)
    for pair in range(blocks // 2):
        x = x_ref[pair_rows(x_ref, first + pair), :]
        turned = turn(x)
        low = low_lanes(x.shape)
        for block, value in ((2 * pair, jnp.where(low, x, turned)), (2 * pair + 1, jnp.where(low, turned, x))):
            left = hi_lo_lanes(value)
            out = jnp.dot(jnp.concatenate([left, left], axis=1), weights[block], preferred_element_type=F32)
            out_ref[:, block * width : (block + 1) * width] = out


VMEM = pl.BlockSpec(memory_space=pltpu.VMEM)
SMEM = pl.BlockSpec(memory_space=pltpu.SMEM)
HBM = pl.BlockSpec(memory_space=pltpu.HBM)


def call(kernel, outs, specs, scratch=(), mib=12, cost=None, out_specs=None, steps=1):
    return pl.pallas_call(
        kernel,
        out_shape=outs,
        grid=(steps,),
        in_specs=specs,
        out_specs=out_specs or [VMEM] * len(outs),
        scratch_shapes=scratch,
        cost_estimate=cost,
        compiler_params=pltpu.CompilerParams(vmem_limit_bytes=mib * 2**20),
    )


def exchange(x):
    rows = x.shape[0]
    x = x.reshape(64, 1, rows * LANES // 64)
    return lax.all_to_all(x, GROUP, 0, 0, tiled=True).reshape(rows, LANES)


def partner(x, axis):
    return lax.ppermute(x, axis, [(0, 1), (1, 0)])


def local(signals, leaf_maps, root_maps, translations, source_list, type_list):
    blocks, rank, width = leaf_maps.shape
    waves = signals.shape[0]
    levels, kinds = translations.shape[:2]
    sources, types = jnp.swapaxes(source_list, 1, 2), jnp.swapaxes(type_list, 1, 2)
    root_maps = jnp.swapaxes(root_maps, 1, 2)
    held = pltpu.VMEM((blocks, waves, LANES), BF16)
    flat = jax.ShapeDtypeStruct((waves * blocks // 2, LANES), F32)
    other, left = call(
        start_kernel,
        [flat, jax.ShapeDtypeStruct((blocks, waves, LANES), BF16)],
        [SMEM, SMEM, HBM, HBM, HBM],
        [
            held,
            pltpu.VMEM((kinds, 2 * rank, LANES), BF16),
            pltpu.VMEM((kinds, rank, rank), F32),
            pltpu.VMEM((waves, blocks * width), F32),
            pltpu.VMEM((blocks, rank, width), F32),
            pltpu.SemaphoreType.DMA((3, 3)),
        ],
        mib=60,
        out_specs=[VMEM, HBM],
    )(sources, types, translations, signals, leaf_maps)
    received = partner(other, "y0")

    def prepared(count):
        return jax.ShapeDtypeStruct((count, kinds, 2 * rank, LANES), BF16)

    own, early, late, root_weights = call(
        prepare_kernel,
        [flat, prepared(4), prepared(3), jax.ShapeDtypeStruct((blocks, 4 * rank, width), BF16)],
        [SMEM, SMEM, VMEM, VMEM, VMEM],
        [pltpu.VMEM((kinds, 2 * rank, LANES), BF16)],
        cost=pl.CostEstimate(flops=2**24, bytes_accessed=2**23, transcendentals=0),
    )(sources, types, translations, root_maps, left)
    x, early, late, root_weights = lax.optimization_barrier((own + received, early, late, root_weights))
    x = exchange(x)
    other, left = call(
        middle_kernel,
        [flat, jax.ShapeDtypeStruct((blocks, waves, LANES), BF16)],
        [SMEM, SMEM, VMEM, VMEM],
        [held, held],
    )(sources, types, early, x)
    received = partner(other, "c")
    (own,) = call(
        own_kernel,
        [flat],
        [SMEM, SMEM, pl.BlockSpec((1, kinds, 2 * rank, LANES), lambda i: (3, 0, 0, 0)), VMEM],
        cost=pl.CostEstimate(flops=2**24, bytes_accessed=2**20, transcendentals=0),
    )(sources, types, early, left)
    (x,) = call(end_kernel, [flat], [SMEM, SMEM, VMEM, VMEM, VMEM], [held, held])(sources, types, late, own, received)
    steps = 3
    (out,) = call(
        root_kernel,
        [jax.ShapeDtypeStruct((waves, blocks * width), F32)],
        [
            pl.BlockSpec(flat.shape, lambda i: (0, 0)),
            pl.BlockSpec((blocks // steps, 4 * rank, width), lambda i: (i, 0, 0)),
        ],
        out_specs=[pl.BlockSpec((waves, blocks // steps * width), lambda i: (0, i))],
        steps=steps,
    )(exchange(x), root_weights)
    return out


def solution(mesh):
    fine = Mesh(mesh.devices.reshape((2,) * len(BITS)), BITS)
    placed = (P(None, BITS), P(BITS, None, None), P(BITS, None, None), P(), P(), P())
    return jax.shard_map(local, mesh=fine, in_specs=placed, out_specs=P(None, BITS), check_vma=False)
```

```python
import functools

import jax
import jax.numpy as jnp
from jax import lax
from jax.experimental import pallas as pl
from jax.experimental.pallas import tpu as pltpu
from jax.sharding import Mesh, PartitionSpec as P

BITS = ("z1", "z0", "y1", "y0", "x1", "x0", "zh", "c")
GROUP = ("z1", "z0", "y1", "x1", "x0", "zh")
FLIPS = ("y0", "y1", "z0", "z1", "c", "zh", "x0", "x1")
LANES = 128
F32, BF16 = jnp.float32, jnp.bfloat16
NT = (((1,), (1,)), ((), ()))


def row_mask(level):
    return 1 << (len(GROUP) - 1 - GROUP.index(FLIPS[level]))


def dot_nt(a, b):
    return lax.dot_general(a, b, NT, preferred_element_type=F32)


def split(x):
    hi = x.astype(BF16)
    return hi, (x - hi.astype(F32)).astype(BF16)


def low_lanes(shape):
    return lax.broadcasted_iota(jnp.int32, shape, 1) < LANES // 2


def turn(x):
    return pltpu.roll(x, LANES // 2, 1)


def hi_lo_lanes(x):
    hi = x.astype(BF16).astype(F32)
    return jnp.where(low_lanes(x.shape), hi, x - hi).astype(BF16)


def flip_rows(v, mask):
    groups = [v[8 * i : 8 * i + 8] for i in range(v.shape[0] // 8)]
    if mask >= 8:
        groups = [groups[i ^ (mask // 8)] for i in range(len(groups))]
    elif mask == 4:
        groups = [pltpu.roll(g, 4, 0) for g in groups]
    else:
        bit = (lax.broadcasted_iota(jnp.int32, (8, LANES), 0) & mask) != 0
        groups = [jnp.where(bit, pltpu.roll(g, mask, 0), pltpu.roll(g, 8 - mask, 0)) for g in groups]
    return jnp.concatenate(groups, axis=0)


def pair_rows(ref, pair):
    return pl.ds(pair, ref.shape[0] // 12, stride=12)


def put_pair(held, pair, x):
    turned = turn(x)
    low = low_lanes(x.shape)
    held[2 * pair] = hi_lo_lanes(jnp.where(low, x, turned))
    held[2 * pair + 1] = hi_lo_lanes(jnp.where(low, turned, x))


def put_weights(mat, out_ref):
    hi, lo = split(mat.T)
    both = jnp.concatenate([hi, lo], axis=1)
    rank = mat.shape[0]
    out_ref[:rank] = both
    out_ref[rank:] = both


def two_terms(level, block, entry, sources, types, back, held, weights):
    left = [held[sources[level, entry + i, block] - back] for i in range(2)]
    right = [weights[types[level, entry + i, block]] for i in range(2)]
    return jnp.dot(jnp.concatenate(left, axis=1), jnp.concatenate(right, axis=0), preferred_element_type=F32)


def level_step(level, sources, types, held, weights, emit):
    blocks = held.shape[0]

    def pair_step(pair, carry):
        terms = []
        for block in (2 * pair, 2 * pair + 1):
            terms.append(two_terms(level, block, 0, sources, types, 0, held, weights))
            terms.append(two_terms(level, block, 2, sources, types, blocks, held, weights))
        emit(pair, *terms)
        return carry

    lax.fori_loop(0, blocks // 2, pair_step, 0, unroll=True)


def half_level(level, entry, back, sources, types, held, weights, out_ref):
    def pair_step(pair, carry):
        even = two_terms(level, 2 * pair, entry, sources, types, back, held, weights)
        odd = two_terms(level, 2 * pair + 1, entry, sources, types, back, held, weights)
        out_ref[pair_rows(out_ref, pair), :] = join(even, odd)
        return carry

    lax.fori_loop(0, held.shape[0] // 2, pair_step, 0, unroll=True)


def flip_and_keep(held, mask):
    def emit(pair, own_even, other_even, own_odd, other_odd):
        for block, own, other in ((2 * pair, own_even, other_even), (2 * pair + 1, own_odd, other_odd)):
            total = own + flip_rows(other, mask)
            held[block] = hi_lo_lanes(total + turn(total))

    return emit


def flip_and_give(out_ref, mask):
    def emit(pair, own_even, other_even, own_odd, other_odd):
        even = own_even + flip_rows(other_even, mask)
        odd = own_odd + flip_rows(other_odd, mask)
        out_ref[pair_rows(out_ref, pair), :] = join(even, odd)

    return emit


def join(even, odd):
    low = low_lanes(even.shape)
    return jnp.where(low, even, odd) + turn(jnp.where(low, odd, even))


def give_both(own_ref, other_ref):
    def emit(pair, own_even, other_even, own_odd, other_odd):
        own_ref[pair_rows(own_ref, pair), :] = join(own_even, own_odd)
        other_ref[pair_rows(other_ref, pair), :] = join(other_even, other_odd)

    return emit


def run_levels(first, count, sources, types, held, weights, last):
    for i in range(count):
        now, then = held[i % 2], held[(i + 1) % 2]
        emit = last if i == count - 1 else flip_and_keep(then, row_mask(first + i))
        level_step(first + i, sources, types, now, weights.at[i], emit)


def start_kernel(
    sources, types, tables, signals, maps, other_ref, held, weights, table_in, signals_in, maps_in, sems
):
    blocks, rank, width = maps.shape
    parts = sems.shape[1]
    some = blocks // parts
    table_copy = pltpu.make_async_copy(tables.at[0], table_in, sems.at[2, 0])
    table_copy.start()
    copies = []
    for i in range(parts):
        lanes, rows = pl.ds(i * some * width, some * width), pl.ds(i * some, some)
        copies.append(
            (
                pltpu.make_async_copy(signals.at[:, lanes], signals_in.at[:, lanes], sems.at[0, i]),
                pltpu.make_async_copy(maps.at[rows], maps_in.at[rows], sems.at[1, i]),
            )
        )
        for copy in copies[-1]:
            copy.start()
    table_copy.wait()
    for kind in range(weights.shape[0]):
        put_weights(table_in[kind], weights.at[kind])

    def leaf(k, carry):
        wave_hi, wave_lo = split(signals_in[:, pl.ds(pl.multiple_of(k * width, width), width)])
        map_hi, map_lo = split(maps_in[k])
        left = jnp.concatenate([wave_hi, wave_lo], axis=1)
        both = jnp.concatenate([map_hi, map_lo], axis=0)
        total = dot_nt(left, jnp.concatenate([both, both], axis=1))
        held[k] = hi_lo_lanes(total + turn(total))
        return carry

    for i in range(parts):
        for copy in copies[i]:
            copy.wait()
        lax.fori_loop(i * some, (i + 1) * some, leaf, 0, unroll=some)
    half_level(0, 2, blocks, sources, types, held, weights, other_ref)


def prepare_kernel(sources, types, tables, maps, held, own_ref, early, late, root_weights, weights_here):
    for kind in range(tables.shape[1]):
        put_weights(tables[0, kind], weights_here.at[kind])
    half_level(0, 0, 0, sources, types, held, weights_here, own_ref)

    for first, weights in ((1, early), (1 + early.shape[0], late)):

        def table(level, carry, first=first, weights=weights):
            for kind in range(tables.shape[1]):
                put_weights(tables[first + level, kind], weights.at[level, kind])
            return carry

        lax.fori_loop(0, weights.shape[0], table, 0)

    def root(block, carry):
        hi, lo = split(maps[block])
        root_weights[block] = jnp.concatenate([hi, hi, lo, lo], axis=0)
        return carry

    lax.fori_loop(0, maps.shape[0], root, 0, unroll=4)


def middle_kernel(sources, types, weights, x_ref, other_ref, left_ref, held, held_too):
    blocks = held.shape[0]
    for pair in range(blocks // 2):
        put_pair(held, pair, x_ref[pair_rows(x_ref, pair), :])
    run_levels(1, 3, sources, types, (held, held_too), weights, flip_and_keep(left_ref, row_mask(3)))
    half_level(4, 2, blocks, sources, types, left_ref, weights.at[3], other_ref)


def own_kernel(sources, types, weights, left, own_ref):
    half_level(4, 0, 0, sources, types, left, weights.at[0], own_ref)


def end_kernel(sources, types, weights, own_ref, other_ref, out_ref, held, held_too):
    for pair in range(held.shape[0] // 2):
        rows = pair_rows(own_ref, pair)
        put_pair(held, pair, own_ref[rows, :] + other_ref[rows, :])
    run_levels(5, 3, sources, types, (held, held_too), weights, flip_and_give(out_ref, row_mask(7)))


def root_kernel(x_ref, weights, out_ref):
    blocks, width = weights.shape[0], weights.shape[2]

    def body(pair, carry):
        x = x_ref[pair_rows(x_ref, pair), :]
        turned = turn(x)
        low = low_lanes(x.shape)
        for block, value in ((2 * pair, jnp.where(low, x, turned)), (2 * pair + 1, jnp.where(low, turned, x))):
            left = hi_lo_lanes(value)
            out = jnp.dot(jnp.concatenate([left, left], axis=1), weights[block], preferred_element_type=F32)
            out_ref[:, pl.ds(pl.multiple_of(block * width, width), width)] = out
        return carry

    lax.fori_loop(0, blocks // 2, body, 0, unroll=4)


VMEM = pl.BlockSpec(memory_space=pltpu.VMEM)
SMEM = pl.BlockSpec(memory_space=pltpu.SMEM)
HBM = pl.BlockSpec(memory_space=pltpu.HBM)


def call(kernel, outs, specs, scratch=(), mib=12, cost=None):
    return pl.pallas_call(
        kernel,
        out_shape=outs,
        grid=(1,),
        in_specs=specs,
        out_specs=[VMEM] * len(outs),
        scratch_shapes=scratch,
        cost_estimate=cost,
        compiler_params=pltpu.CompilerParams(vmem_limit_bytes=mib * 2**20),
    )


def exchange(x):
    rows = x.shape[0]
    x = x.reshape(64, 1, rows * LANES // 64)
    return lax.all_to_all(x, GROUP, 0, 0, tiled=True).reshape(rows, LANES)


def partner(x, axis):
    return lax.ppermute(x, axis, [(0, 1), (1, 0)])


def local(signals, leaf_maps, root_maps, translations, source_list, type_list):
    blocks, rank, width = leaf_maps.shape
    waves = signals.shape[0]
    levels, kinds = translations.shape[:2]
    sources, types = jnp.swapaxes(source_list, 1, 2), jnp.swapaxes(type_list, 1, 2)
    root_maps = jnp.swapaxes(root_maps, 1, 2)
    held = pltpu.VMEM((blocks, waves, LANES), BF16)
    flat = jax.ShapeDtypeStruct((waves * blocks // 2, LANES), F32)
    other, left = call(
        start_kernel,
        [flat, jax.ShapeDtypeStruct((blocks, waves, LANES), BF16)],
        [SMEM, SMEM, HBM, HBM, HBM],
        [
            pltpu.VMEM((kinds, 2 * rank, LANES), BF16),
            pltpu.VMEM((kinds, rank, rank), F32),
            pltpu.VMEM((waves, blocks * width), F32),
            pltpu.VMEM((blocks, rank, width), F32),
            pltpu.SemaphoreType.DMA((3, 3)),
        ],
        mib=60,
    )(sources, types, translations, signals, leaf_maps)
    other, translations, root_maps = lax.optimization_barrier((other, translations, root_maps))
    received = partner(other, "y0")

    def prepared(count):
        return jax.ShapeDtypeStruct((count, kinds, 2 * rank, LANES), BF16)

    own, early, late, root_weights = call(
        prepare_kernel,
        [flat, prepared(4), prepared(3), jax.ShapeDtypeStruct((blocks, 4 * rank, width), BF16)],
        [SMEM, SMEM, VMEM, VMEM, VMEM],
        [pltpu.VMEM((kinds, 2 * rank, LANES), BF16)],
        cost=pl.CostEstimate(flops=2**24, bytes_accessed=2**23, transcendentals=0),
    )(sources, types, translations, root_maps, left)
    x, early, late, root_weights = lax.optimization_barrier((own + received, early, late, root_weights))
    x = exchange(x)
    other, left = call(
        middle_kernel,
        [flat, jax.ShapeDtypeStruct((blocks, waves, LANES), BF16)],
        [SMEM, SMEM, VMEM, VMEM],
        [held, held],
    )(sources, types, early, x)
    received = partner(other, "c")
    (own,) = call(
        own_kernel,
        [flat],
        [SMEM, SMEM, pl.BlockSpec((1, kinds, 2 * rank, LANES), lambda i: (3, 0, 0, 0)), VMEM],
        cost=pl.CostEstimate(flops=2**24, bytes_accessed=2**20, transcendentals=0),
    )(sources, types, early, left)
    (x,) = call(end_kernel, [flat], [SMEM, SMEM, VMEM, VMEM, VMEM], [held, held])(sources, types, late, own, received)
    (out,) = call(root_kernel, [jax.ShapeDtypeStruct((waves, blocks * width), F32)], [VMEM, VMEM])(
        exchange(x), root_weights
    )
    return out


def solution(mesh):
    fine = Mesh(mesh.devices.reshape((2,) * len(BITS)), BITS)
    placed = (P(None, BITS), P(BITS, None, None), P(BITS, None, None), P(), P(), P())
    return jax.shard_map(local, mesh=fine, in_specs=placed, out_specs=P(None, BITS), check_vma=False)
```

```python
import functools

import jax
import jax.numpy as jnp
from jax import lax
from jax.experimental import pallas as pl
from jax.experimental.pallas import tpu as pltpu
from jax.sharding import Mesh, PartitionSpec as P

BITS = ("z1", "z0", "y1", "y0", "x1", "x0", "zh", "c")
GROUP = ("z1", "z0", "y1", "x1", "x0", "zh")
FLIPS = ("y0", "y1", "z0", "z1", "c", "zh", "x0", "x1")
LANES = 128
F32, BF16 = jnp.float32, jnp.bfloat16
NT = (((1,), (1,)), ((), ()))


def row_mask(level):
    return 1 << (len(GROUP) - 1 - GROUP.index(FLIPS[level]))


def dot_nt(a, b):
    return lax.dot_general(a, b, NT, preferred_element_type=F32)


def split(x):
    hi = x.astype(BF16)
    return hi, (x - hi.astype(F32)).astype(BF16)


def low_lanes(shape):
    return lax.broadcasted_iota(jnp.int32, shape, 1) < LANES // 2


def turn(x):
    return pltpu.roll(x, LANES // 2, 1)


def hi_lo_lanes(x):
    hi = x.astype(BF16).astype(F32)
    return jnp.where(low_lanes(x.shape), hi, x - hi).astype(BF16)


def flip_rows(v, mask):
    groups = [v[8 * i : 8 * i + 8] for i in range(v.shape[0] // 8)]
    if mask >= 8:
        groups = [groups[i ^ (mask // 8)] for i in range(len(groups))]
    elif mask == 4:
        groups = [pltpu.roll(g, 4, 0) for g in groups]
    else:
        bit = (lax.broadcasted_iota(jnp.int32, (8, LANES), 0) & mask) != 0
        groups = [jnp.where(bit, pltpu.roll(g, mask, 0), pltpu.roll(g, 8 - mask, 0)) for g in groups]
    return jnp.concatenate(groups, axis=0)


def pair_rows(ref, pair):
    return pl.ds(pair, ref.shape[0] // 12, stride=12)


def put_pair(held, pair, x):
    turned = turn(x)
    low = low_lanes(x.shape)
    held[2 * pair] = hi_lo_lanes(jnp.where(low, x, turned))
    held[2 * pair + 1] = hi_lo_lanes(jnp.where(low, turned, x))


def put_weights(mat, out_ref):
    hi, lo = split(mat.T)
    out_ref[...] = jnp.concatenate([hi, lo], axis=1)


def two_terms(level, block, entry, sources, types, back, held, weights):
    left = [held[sources[level, entry + i, block] - back] for i in range(2)]
    right = [weights[types[level, entry + i, block]] for i in range(2)]
    right = [right[0], right[0], right[1], right[1]]
    return jnp.dot(jnp.concatenate(left, axis=1), jnp.concatenate(right, axis=0), preferred_element_type=F32)


def level_step(level, sources, types, held, weights, emit):
    blocks = held.shape[0]

    def pair_step(pair, carry):
        terms = []
        for block in (2 * pair, 2 * pair + 1):
            terms.append(two_terms(level, block, 0, sources, types, 0, held, weights))
            terms.append(two_terms(level, block, 2, sources, types, blocks, held, weights))
        emit(pair, *terms)
        return carry

    lax.fori_loop(0, blocks // 2, pair_step, 0, unroll=True)


def half_level(level, entry, back, sources, types, held, weights, out_ref):
    def pair_step(pair, carry):
        even = two_terms(level, 2 * pair, entry, sources, types, back, held, weights)
        odd = two_terms(level, 2 * pair + 1, entry, sources, types, back, held, weights)
        out_ref[pair_rows(out_ref, pair), :] = join(even, odd)
        return carry

    lax.fori_loop(0, held.shape[0] // 2, pair_step, 0, unroll=True)


def flip_and_keep(held, mask):
    def emit(pair, own_even, other_even, own_odd, other_odd):
        for block, own, other in ((2 * pair, own_even, other_even), (2 * pair + 1, own_odd, other_odd)):
            total = own + flip_rows(other, mask)
            held[block] = hi_lo_lanes(total + turn(total))

    return emit


def flip_and_give(out_ref, mask):
    def emit(pair, own_even, other_even, own_odd, other_odd):
        even = own_even + flip_rows(other_even, mask)
        odd = own_odd + flip_rows(other_odd, mask)
        out_ref[pair_rows(out_ref, pair), :] = join(even, odd)

    return emit


def join(even, odd):
    low = low_lanes(even.shape)
    return jnp.where(low, even, odd) + turn(jnp.where(low, odd, even))


def give_both(own_ref, other_ref):
    def emit(pair, own_even, other_even, own_odd, other_odd):
        own_ref[pair_rows(own_ref, pair), :] = join(own_even, own_odd)
        other_ref[pair_rows(other_ref, pair), :] = join(other_even, other_odd)

    return emit


def run_levels(first, count, sources, types, held, weights, last):
    for i in range(count):
        now, then = held[i % 2], held[(i + 1) % 2]
        emit = last if i == count - 1 else flip_and_keep(then, row_mask(first + i))
        level_step(first + i, sources, types, now, weights.at[i], emit)


def start_kernel(
    sources, types, tables, signals, maps, other_ref, held, weights, table_in, signals_in, maps_in, sems
):
    blocks, rank, width = maps.shape
    parts = sems.shape[1]
    some = blocks // parts
    table_copy = pltpu.make_async_copy(tables.at[0], table_in, sems.at[2, 0])
    table_copy.start()
    copies = []
    for i in range(parts):
        lanes, rows = pl.ds(i * some * width, some * width), pl.ds(i * some, some)
        copies.append(
            (
                pltpu.make_async_copy(signals.at[:, lanes], signals_in.at[:, lanes], sems.at[0, i]),
                pltpu.make_async_copy(maps.at[rows], maps_in.at[rows], sems.at[1, i]),
            )
        )
        for copy in copies[-1]:
            copy.start()
    table_copy.wait()
    for kind in range(weights.shape[0]):
        put_weights(table_in[kind], weights.at[kind])

    def leaf(k, carry):
        wave_hi, wave_lo = split(signals_in[:, pl.ds(pl.multiple_of(k * width, width), width)])
        map_hi, map_lo = split(maps_in[k])
        left = jnp.concatenate([wave_hi, wave_lo], axis=1)
        both = jnp.concatenate([map_hi, map_lo], axis=0)
        total = dot_nt(left, jnp.concatenate([both, both], axis=1))
        held[k] = hi_lo_lanes(total + turn(total))
        return carry

    for i in range(parts):
        for copy in copies[i]:
            copy.wait()
        lax.fori_loop(i * some, (i + 1) * some, leaf, 0, unroll=some)
    half_level(0, 2, blocks, sources, types, held, weights, other_ref)


def prepare_kernel(sources, types, tables, maps, held, own_ref, early, late, root_weights, weights_here):
    for kind in range(tables.shape[1]):
        put_weights(tables[0, kind], weights_here.at[kind])
    half_level(0, 0, 0, sources, types, held, weights_here, own_ref)

    for first, weights in ((1, early), (1 + early.shape[0], late)):

        def table(level, carry, first=first, weights=weights):
            for kind in range(tables.shape[1]):
                put_weights(tables[first + level, kind], weights.at[level, kind])
            return carry

        lax.fori_loop(0, weights.shape[0], table, 0)

    def root(block, carry):
        hi, lo = split(maps[block])
        root_weights[block] = jnp.concatenate([hi, lo], axis=0)
        return carry

    lax.fori_loop(0, maps.shape[0], root, 0, unroll=4)


def middle_kernel(sources, types, weights, x_ref, other_ref, left_ref, held, held_too):
    blocks = held.shape[0]
    for pair in range(blocks // 2):
        put_pair(held, pair, x_ref[pair_rows(x_ref, pair), :])
    run_levels(1, 3, sources, types, (held, held_too), weights, flip_and_keep(left_ref, row_mask(3)))
    half_level(4, 2, blocks, sources, types, left_ref, weights.at[3], other_ref)


def own_kernel(sources, types, weights, left, own_ref):
    half_level(4, 0, 0, sources, types, left, weights.at[0], own_ref)


def end_kernel(sources, types, weights, own_ref, other_ref, out_ref, held, held_too):
    for pair in range(held.shape[0] // 2):
        rows = pair_rows(own_ref, pair)
        put_pair(held, pair, own_ref[rows, :] + other_ref[rows, :])
    run_levels(5, 3, sources, types, (held, held_too), weights, flip_and_give(out_ref, row_mask(7)))


def root_kernel(x_ref, weights, out_ref):
    blocks, rank, width = weights.shape[0], weights.shape[1] // 2, weights.shape[2]

    def body(pair, carry):
        x = x_ref[pair_rows(x_ref, pair), :]
        turned = turn(x)
        low = low_lanes(x.shape)
        for block, value in ((2 * pair, jnp.where(low, x, turned)), (2 * pair + 1, jnp.where(low, turned, x))):
            left = hi_lo_lanes(value)
            hi, lo = weights[block, :rank], weights[block, rank:]
            right = jnp.concatenate([hi, hi, lo, lo], axis=0)
            out = jnp.dot(jnp.concatenate([left, left], axis=1), right, preferred_element_type=F32)
            out_ref[:, pl.ds(pl.multiple_of(block * width, width), width)] = out
        return carry

    lax.fori_loop(0, blocks // 2, body, 0, unroll=4)


VMEM = pl.BlockSpec(memory_space=pltpu.VMEM)
SMEM = pl.BlockSpec(memory_space=pltpu.SMEM)
HBM = pl.BlockSpec(memory_space=pltpu.HBM)


def call(kernel, outs, specs, scratch=(), mib=12, cost=None):
    return pl.pallas_call(
        kernel,
        out_shape=outs,
        grid=(1,),
        in_specs=specs,
        out_specs=[VMEM] * len(outs),
        scratch_shapes=scratch,
        cost_estimate=cost,
        compiler_params=pltpu.CompilerParams(vmem_limit_bytes=mib * 2**20),
    )


def exchange(x):
    rows = x.shape[0]
    x = x.reshape(64, 1, rows * LANES // 64)
    return lax.all_to_all(x, GROUP, 0, 0, tiled=True).reshape(rows, LANES)


def partner(x, axis):
    return lax.ppermute(x, axis, [(0, 1), (1, 0)])


def local(signals, leaf_maps, root_maps, translations, source_list, type_list):
    blocks, rank, width = leaf_maps.shape
    waves = signals.shape[0]
    levels, kinds = translations.shape[:2]
    sources, types = jnp.swapaxes(source_list, 1, 2), jnp.swapaxes(type_list, 1, 2)
    root_maps = jnp.swapaxes(root_maps, 1, 2)
    held = pltpu.VMEM((blocks, waves, LANES), BF16)
    flat = jax.ShapeDtypeStruct((waves * blocks // 2, LANES), F32)
    other, left = call(
        start_kernel,
        [flat, jax.ShapeDtypeStruct((blocks, waves, LANES), BF16)],
        [SMEM, SMEM, HBM, HBM, HBM],
        [
            pltpu.VMEM((kinds, rank, LANES), BF16),
            pltpu.VMEM((kinds, rank, rank), F32),
            pltpu.VMEM((waves, blocks * width), F32),
            pltpu.VMEM((blocks, rank, width), F32),
            pltpu.SemaphoreType.DMA((3, 3)),
        ],
        mib=60,
    )(sources, types, translations, signals, leaf_maps)
    other, translations, root_maps = lax.optimization_barrier((other, translations, root_maps))
    received = partner(other, "y0")

    def prepared(count):
        return jax.ShapeDtypeStruct((count, kinds, rank, LANES), BF16)

    own, early, late, root_weights = call(
        prepare_kernel,
        [flat, prepared(4), prepared(3), jax.ShapeDtypeStruct((blocks, 2 * rank, width), BF16)],
        [SMEM, SMEM, VMEM, VMEM, VMEM],
        [pltpu.VMEM((kinds, rank, LANES), BF16)],
        cost=pl.CostEstimate(flops=2**24, bytes_accessed=2**23, transcendentals=0),
    )(sources, types, translations, root_maps, left)
    x, early, late, root_weights = lax.optimization_barrier((own + received, early, late, root_weights))
    x = exchange(x)
    other, left = call(
        middle_kernel,
        [flat, jax.ShapeDtypeStruct((blocks, waves, LANES), BF16)],
        [SMEM, SMEM, VMEM, VMEM],
        [held, held],
    )(sources, types, early, x)
    received = partner(other, "c")
    (own,) = call(
        own_kernel,
        [flat],
        [SMEM, SMEM, pl.BlockSpec((1, kinds, rank, LANES), lambda i: (3, 0, 0, 0)), VMEM],
        cost=pl.CostEstimate(flops=2**24, bytes_accessed=2**20, transcendentals=0),
    )(sources, types, early, left)
    (x,) = call(end_kernel, [flat], [SMEM, SMEM, VMEM, VMEM, VMEM], [held, held])(sources, types, late, own, received)
    (out,) = call(root_kernel, [jax.ShapeDtypeStruct((waves, blocks * width), F32)], [VMEM, VMEM])(
        exchange(x), root_weights
    )
    return out


def solution(mesh):
    fine = Mesh(mesh.devices.reshape((2,) * len(BITS)), BITS)
    placed = (P(None, BITS), P(BITS, None, None), P(BITS, None, None), P(), P(), P())
    return jax.shard_map(local, mesh=fine, in_specs=placed, out_specs=P(None, BITS), check_vma=False)
```

```python
import functools

import jax
import jax.numpy as jnp
from jax import lax
from jax.experimental import pallas as pl
from jax.experimental.pallas import tpu as pltpu
from jax.sharding import Mesh, PartitionSpec as P

BITS = ("z1", "z0", "y1", "y0", "x1", "x0", "zh", "c")
GROUP = ("z1", "z0", "y1", "x1", "x0", "zh")
FLIPS = ("y0", "y1", "z0", "z1", "c", "zh", "x0", "x1")
LANES = 128
F32, BF16 = jnp.float32, jnp.bfloat16
NT = (((1,), (1,)), ((), ()))


def row_mask(level):
    return 1 << (len(GROUP) - 1 - GROUP.index(FLIPS[level]))


def dot_nt(a, b):
    return lax.dot_general(a, b, NT, preferred_element_type=F32)


def split(x):
    hi = x.astype(BF16)
    return hi, (x - hi.astype(F32)).astype(BF16)


def low_lanes(shape):
    return lax.broadcasted_iota(jnp.int32, shape, 1) < LANES // 2


def turn(x):
    return pltpu.roll(x, LANES // 2, 1)


def hi_lo_lanes(x):
    hi = x.astype(BF16).astype(F32)
    return jnp.where(low_lanes(x.shape), hi, x - hi).astype(BF16)


def flip_rows(v, mask):
    groups = [v[8 * i : 8 * i + 8] for i in range(v.shape[0] // 8)]
    if mask >= 8:
        groups = [groups[i ^ (mask // 8)] for i in range(len(groups))]
    elif mask == 4:
        groups = [pltpu.roll(g, 4, 0) for g in groups]
    else:
        bit = (lax.broadcasted_iota(jnp.int32, (8, LANES), 0) & mask) != 0
        groups = [jnp.where(bit, pltpu.roll(g, mask, 0), pltpu.roll(g, 8 - mask, 0)) for g in groups]
    return jnp.concatenate(groups, axis=0)


def pair_rows(ref, pair):
    return pl.ds(pair, ref.shape[0] // 12, stride=12)


def put_pair(held, pair, x):
    turned = turn(x)
    low = low_lanes(x.shape)
    held[2 * pair] = hi_lo_lanes(jnp.where(low, x, turned))
    held[2 * pair + 1] = hi_lo_lanes(jnp.where(low, turned, x))


def put_weights(mat, out_ref):
    hi, lo = split(mat.T)
    out_ref[...] = jnp.concatenate([hi, lo], axis=1)


def two_terms(level, block, entry, sources, types, back, held, weights):
    left = [held[sources[level, entry + i, block] - back] for i in range(2)]
    right = [weights[types[level, entry + i, block]] for i in range(2)]
    right = [right[0], right[0], right[1], right[1]]
    return jnp.dot(jnp.concatenate(left, axis=1), jnp.concatenate(right, axis=0), preferred_element_type=F32)


def level_step(level, sources, types, held, weights, emit):
    blocks = held.shape[0]

    def pair_step(pair, carry):
        terms = []
        for block in (2 * pair, 2 * pair + 1):
            terms.append(two_terms(level, block, 0, sources, types, 0, held, weights))
            terms.append(two_terms(level, block, 2, sources, types, blocks, held, weights))
        emit(pair, *terms)
        return carry

    lax.fori_loop(0, blocks // 2, pair_step, 0, unroll=True)


def half_level(level, entry, back, sources, types, held, weights, out_ref):
    def pair_step(pair, carry):
        even = two_terms(level, 2 * pair, entry, sources, types, back, held, weights)
        odd = two_terms(level, 2 * pair + 1, entry, sources, types, back, held, weights)
        out_ref[pair_rows(out_ref, pair), :] = join(even, odd)
        return carry

    lax.fori_loop(0, held.shape[0] // 2, pair_step, 0, unroll=True)


def flip_and_keep(held, mask):
    def emit(pair, own_even, other_even, own_odd, other_odd):
        for block, own, other in ((2 * pair, own_even, other_even), (2 * pair + 1, own_odd, other_odd)):
            total = own + flip_rows(other, mask)
            held[block] = hi_lo_lanes(total + turn(total))

    return emit


def flip_and_give(out_ref, mask):
    def emit(pair, own_even, other_even, own_odd, other_odd):
        even = own_even + flip_rows(other_even, mask)
        odd = own_odd + flip_rows(other_odd, mask)
        out_ref[pair_rows(out_ref, pair), :] = join(even, odd)

    return emit


def join(even, odd):
    low = low_lanes(even.shape)
    return jnp.where(low, even, odd) + turn(jnp.where(low, odd, even))


def give_both(own_ref, other_ref):
    def emit(pair, own_even, other_even, own_odd, other_odd):
        own_ref[pair_rows(own_ref, pair), :] = join(own_even, own_odd)
        other_ref[pair_rows(other_ref, pair), :] = join(other_even, other_odd)

    return emit


def run_levels(first, count, sources, types, held, weights, last):
    for i in range(count):
        now, then = held[i % 2], held[(i + 1) % 2]
        emit = last if i == count - 1 else flip_and_keep(then, row_mask(first + i))
        level_step(first + i, sources, types, now, weights.at[i], emit)


def start_kernel(
    sources, types, tables, signals, maps, other_ref, held, weights, table_in, signals_in, maps_in, sems
):
    blocks, rank, width = maps.shape
    parts = sems.shape[1]
    some = blocks // parts
    table_copy = pltpu.make_async_copy(tables.at[0], table_in, sems.at[2, 0])
    table_copy.start()
    copies = []
    for i in range(parts):
        lanes, rows = pl.ds(i * some * width, some * width), pl.ds(i * some, some)
        copies.append(
            (
                pltpu.make_async_copy(signals.at[:, lanes], signals_in.at[:, lanes], sems.at[0, i]),
                pltpu.make_async_copy(maps.at[rows], maps_in.at[rows], sems.at[1, i]),
            )
        )
        for copy in copies[-1]:
            copy.start()
    table_copy.wait()
    for kind in range(weights.shape[0]):
        put_weights(table_in[kind], weights.at[kind])

    def leaf(k, carry):
        wave_hi, wave_lo = split(signals_in[:, pl.ds(pl.multiple_of(k * width, width), width)])
        map_hi, map_lo = split(maps_in[k])
        left = jnp.concatenate([wave_hi, wave_lo], axis=1)
        both = jnp.concatenate([map_hi, map_lo], axis=0)
        total = dot_nt(left, jnp.concatenate([both, both], axis=1))
        held[k] = hi_lo_lanes(total + turn(total))
        return carry

    for i in range(parts):
        for copy in copies[i]:
            copy.wait()
        lax.fori_loop(i * some, (i + 1) * some, leaf, 0, unroll=some)
    half_level(0, 2, blocks, sources, types, held, weights, other_ref)


def prepare_kernel(sources, types, tables, maps, held, own_ref, early, late, root_weights, weights_here):
    for kind in range(tables.shape[1]):
        put_weights(tables[0, kind], weights_here.at[kind])
    half_level(0, 0, 0, sources, types, held, weights_here, own_ref)

    for first, weights in ((1, early), (1 + early.shape[0], late)):

        def table(level, carry, first=first, weights=weights):
            for kind in range(tables.shape[1]):
                put_weights(tables[first + level, kind], weights.at[level, kind])
            return carry

        lax.fori_loop(0, weights.shape[0], table, 0)

    def root(block, carry):
        hi, lo = split(maps[block])
        root_weights[block] = jnp.concatenate([hi, lo], axis=0)
        return carry

    lax.fori_loop(0, maps.shape[0], root, 0, unroll=4)


def middle_kernel(sources, types, weights, x_ref, other_ref, left_ref, held, held_too):
    blocks = held.shape[0]
    for pair in range(blocks // 2):
        put_pair(held, pair, x_ref[pair_rows(x_ref, pair), :])
    run_levels(1, 3, sources, types, (held, held_too), weights, flip_and_keep(left_ref, row_mask(3)))
    half_level(4, 2, blocks, sources, types, left_ref, weights.at[3], other_ref)


def own_kernel(sources, types, weights, left, own_ref):
    half_level(4, 0, 0, sources, types, left, weights.at[0], own_ref)


def end_kernel(sources, types, weights, own_ref, other_ref, out_ref, held, held_too):
    for pair in range(held.shape[0] // 2):
        rows = pair_rows(own_ref, pair)
        put_pair(held, pair, own_ref[rows, :] + other_ref[rows, :])
    run_levels(5, 3, sources, types, (held, held_too), weights, flip_and_give(out_ref, row_mask(7)))


def root_kernel(x_ref, weights, out_ref):
    blocks, rank, width = weights.shape[0], weights.shape[1] // 2, weights.shape[2]

    def body(pair, carry):
        x = x_ref[pair_rows(x_ref, pair), :]
        turned = turn(x)
        low = low_lanes(x.shape)
        for block, value in ((2 * pair, jnp.where(low, x, turned)), (2 * pair + 1, jnp.where(low, turned, x))):
            left = hi_lo_lanes(value)
            hi, lo = weights[block, :rank], weights[block, rank:]
            right = jnp.concatenate([hi, hi, lo, lo], axis=0)
            out = jnp.dot(jnp.concatenate([left, left], axis=1), right, preferred_element_type=F32)
            out_ref[:, pl.ds(pl.multiple_of(block * width, width), width)] = out
        return carry

    lax.fori_loop(0, blocks // 2, body, 0, unroll=True)


VMEM = pl.BlockSpec(memory_space=pltpu.VMEM)
SMEM = pl.BlockSpec(memory_space=pltpu.SMEM)
HBM = pl.BlockSpec(memory_space=pltpu.HBM)


def call(kernel, outs, specs, scratch=(), mib=12, cost=None):
    return pl.pallas_call(
        kernel,
        out_shape=outs,
        grid=(1,),
        in_specs=specs,
        out_specs=[VMEM] * len(outs),
        scratch_shapes=scratch,
        cost_estimate=cost,
        compiler_params=pltpu.CompilerParams(vmem_limit_bytes=mib * 2**20),
    )


def exchange(x):
    rows = x.shape[0]
    x = x.reshape(64, 1, rows * LANES // 64)
    return lax.all_to_all(x, GROUP, 0, 0, tiled=True).reshape(rows, LANES)


def partner(x, axis):
    return lax.ppermute(x, axis, [(0, 1), (1, 0)])


def local(signals, leaf_maps, root_maps, translations, source_list, type_list):
    blocks, rank, width = leaf_maps.shape
    waves = signals.shape[0]
    levels, kinds = translations.shape[:2]
    sources, types = jnp.swapaxes(source_list, 1, 2), jnp.swapaxes(type_list, 1, 2)
    root_maps = jnp.swapaxes(root_maps, 1, 2)
    held = pltpu.VMEM((blocks, waves, LANES), BF16)
    flat = jax.ShapeDtypeStruct((waves * blocks // 2, LANES), F32)
    other, left = call(
        start_kernel,
        [flat, jax.ShapeDtypeStruct((blocks, waves, LANES), BF16)],
        [SMEM, SMEM, HBM, HBM, HBM],
        [
            pltpu.VMEM((kinds, rank, LANES), BF16),
            pltpu.VMEM((kinds, rank, rank), F32),
            pltpu.VMEM((waves, blocks * width), F32),
            pltpu.VMEM((blocks, rank, width), F32),
            pltpu.SemaphoreType.DMA((3, 3)),
        ],
        mib=60,
    )(sources, types, translations, signals, leaf_maps)
    other, translations, root_maps = lax.optimization_barrier((other, translations, root_maps))
    received = partner(other, "y0")

    def prepared(count):
        return jax.ShapeDtypeStruct((count, kinds, rank, LANES), BF16)

    own, early, late, root_weights = call(
        prepare_kernel,
        [flat, prepared(4), prepared(3), jax.ShapeDtypeStruct((blocks, 2 * rank, width), BF16)],
        [SMEM, SMEM, VMEM, VMEM, VMEM],
        [pltpu.VMEM((kinds, rank, LANES), BF16)],
        cost=pl.CostEstimate(flops=2**24, bytes_accessed=2**23, transcendentals=0),
    )(sources, types, translations, root_maps, left)
    x, early, late, root_weights = lax.optimization_barrier((own + received, early, late, root_weights))
    x = exchange(x)
    other, left = call(
        middle_kernel,
        [flat, jax.ShapeDtypeStruct((blocks, waves, LANES), BF16)],
        [SMEM, SMEM, VMEM, VMEM],
        [held, held],
    )(sources, types, early, x)
    received = partner(other, "c")
    (own,) = call(
        own_kernel,
        [flat],
        [SMEM, SMEM, pl.BlockSpec((1, kinds, rank, LANES), lambda i: (3, 0, 0, 0)), VMEM],
        cost=pl.CostEstimate(flops=2**24, bytes_accessed=2**20, transcendentals=0),
    )(sources, types, early, left)
    (x,) = call(end_kernel, [flat], [SMEM, SMEM, VMEM, VMEM, VMEM], [held, held])(sources, types, late, own, received)
    (out,) = call(root_kernel, [jax.ShapeDtypeStruct((waves, blocks * width), F32)], [VMEM, VMEM])(
        exchange(x), root_weights
    )
    return out


def solution(mesh):
    fine = Mesh(mesh.devices.reshape((2,) * len(BITS)), BITS)
    placed = (P(None, BITS), P(BITS, None, None), P(BITS, None, None), P(), P(), P())
    return jax.shard_map(local, mesh=fine, in_specs=placed, out_specs=P(None, BITS), check_vma=False)
```

```python
import functools

import jax
import jax.numpy as jnp
from jax import lax
from jax.experimental import pallas as pl
from jax.experimental.pallas import tpu as pltpu
from jax.sharding import Mesh, PartitionSpec as P

BITS = ("z1", "z0", "y1", "y0", "x1", "x0", "zh", "c")
GROUP = ("z1", "z0", "y1", "x1", "x0", "zh")
FLIPS = ("y0", "y1", "z0", "z1", "c", "zh", "x0", "x1")
LANES = 128
F32, BF16 = jnp.float32, jnp.bfloat16
NT = (((1,), (1,)), ((), ()))


def row_mask(level):
    return 1 << (len(GROUP) - 1 - GROUP.index(FLIPS[level]))


def dot_nt(a, b):
    return lax.dot_general(a, b, NT, preferred_element_type=F32)


def split(x):
    hi = x.astype(BF16)
    return hi, (x - hi.astype(F32)).astype(BF16)


def low_lanes(shape):
    return lax.broadcasted_iota(jnp.int32, shape, 1) < LANES // 2


def turn(x):
    return pltpu.roll(x, LANES // 2, 1)


def hi_lo_lanes(x):
    hi = x.astype(BF16).astype(F32)
    return jnp.where(low_lanes(x.shape), hi, x - hi).astype(BF16)


def flip_rows(v, mask):
    groups = [v[8 * i : 8 * i + 8] for i in range(v.shape[0] // 8)]
    if mask >= 8:
        groups = [groups[i ^ (mask // 8)] for i in range(len(groups))]
    elif mask == 4:
        groups = [pltpu.roll(g, 4, 0) for g in groups]
    else:
        bit = (lax.broadcasted_iota(jnp.int32, (8, LANES), 0) & mask) != 0
        groups = [jnp.where(bit, pltpu.roll(g, mask, 0), pltpu.roll(g, 8 - mask, 0)) for g in groups]
    return jnp.concatenate(groups, axis=0)


def pair_rows(ref, pair):
    return pl.ds(pair, ref.shape[0] // 12, stride=12)


def put_pair(held, pair, x):
    turned = turn(x)
    low = low_lanes(x.shape)
    held[2 * pair] = hi_lo_lanes(jnp.where(low, x, turned))
    held[2 * pair + 1] = hi_lo_lanes(jnp.where(low, turned, x))


def put_weights(mat, out_ref):
    hi, lo = split(mat.T)
    out_ref[...] = jnp.concatenate([hi, lo], axis=1)


def two_terms(level, block, entry, sources, types, back, held, weights):
    left = [held[sources[level, entry + i, block] - back] for i in range(2)]
    right = [weights[types[level, entry + i, block]] for i in range(2)]
    right = [right[0], right[0], right[1], right[1]]
    return jnp.dot(jnp.concatenate(left, axis=1), jnp.concatenate(right, axis=0), preferred_element_type=F32)


def level_step(level, sources, types, held, weights, emit):
    blocks = held.shape[0]

    def pair_step(pair, carry):
        terms = []
        for block in (2 * pair, 2 * pair + 1):
            terms.append(two_terms(level, block, 0, sources, types, 0, held, weights))
            terms.append(two_terms(level, block, 2, sources, types, blocks, held, weights))
        emit(pair, *terms)
        return carry

    lax.fori_loop(0, blocks // 2, pair_step, 0, unroll=True)


def half_level(level, entry, back, sources, types, held, weights, out_ref):
    def pair_step(pair, carry):
        even = two_terms(level, 2 * pair, entry, sources, types, back, held, weights)
        odd = two_terms(level, 2 * pair + 1, entry, sources, types, back, held, weights)
        out_ref[pair_rows(out_ref, pair), :] = join(even, odd)
        return carry

    lax.fori_loop(0, held.shape[0] // 2, pair_step, 0, unroll=True)


def flip_and_keep(held, mask):
    def emit(pair, own_even, other_even, own_odd, other_odd):
        for block, own, other in ((2 * pair, own_even, other_even), (2 * pair + 1, own_odd, other_odd)):
            total = own + flip_rows(other, mask)
            held[block] = hi_lo_lanes(total + turn(total))

    return emit


def flip_and_give(out_ref, mask):
    def emit(pair, own_even, other_even, own_odd, other_odd):
        even = own_even + flip_rows(other_even, mask)
        odd = own_odd + flip_rows(other_odd, mask)
        out_ref[pair_rows(out_ref, pair), :] = join(even, odd)

    return emit


def join(even, odd):
    low = low_lanes(even.shape)
    return jnp.where(low, even, odd) + turn(jnp.where(low, odd, even))


def give_both(own_ref, other_ref):
    def emit(pair, own_even, other_even, own_odd, other_odd):
        own_ref[pair_rows(own_ref, pair), :] = join(own_even, own_odd)
        other_ref[pair_rows(other_ref, pair), :] = join(other_even, other_odd)

    return emit


def run_levels(first, count, sources, types, held, weights, last):
    for i in range(count):
        now, then = held[i % 2], held[(i + 1) % 2]
        emit = last if i == count - 1 else flip_and_keep(then, row_mask(first + i))
        level_step(first + i, sources, types, now, weights.at[i], emit)


def start_kernel(
    sources, types, tables, signals, maps, other_ref, held, weights, table_in, signals_in, maps_in, sems
):
    blocks, rank, width = maps.shape
    parts = sems.shape[1]
    some = blocks // parts
    table_copy = pltpu.make_async_copy(tables.at[0], table_in, sems.at[2, 0])
    table_copy.start()
    copies = []
    for i in range(parts):
        lanes, rows = pl.ds(i * some * width, some * width), pl.ds(i * some, some)
        copies.append(
            (
                pltpu.make_async_copy(signals.at[:, lanes], signals_in.at[:, lanes], sems.at[0, i]),
                pltpu.make_async_copy(maps.at[rows], maps_in.at[rows], sems.at[1, i]),
            )
        )
        for copy in copies[-1]:
            copy.start()
    table_copy.wait()
    for kind in range(weights.shape[0]):
        put_weights(table_in[kind], weights.at[kind])

    def leaf(k, carry):
        wave_hi, wave_lo = split(signals_in[:, pl.ds(pl.multiple_of(k * width, width), width)])
        map_hi, map_lo = split(maps_in[k])
        left = jnp.concatenate([wave_hi, wave_lo], axis=1)
        both = jnp.concatenate([map_hi, map_lo], axis=0)
        total = dot_nt(left, jnp.concatenate([both, both], axis=1))
        held[k] = hi_lo_lanes(total + turn(total))
        return carry

    for i in range(parts):
        for copy in copies[i]:
            copy.wait()
        lax.fori_loop(i * some, (i + 1) * some, leaf, 0, unroll=some)
    half_level(0, 2, blocks, sources, types, held, weights, other_ref)


def prepare_kernel(sources, types, tables, maps, held, own_ref, early, late, root_weights, weights_here):
    for kind in range(tables.shape[1]):
        put_weights(tables[0, kind], weights_here.at[kind])
    half_level(0, 0, 0, sources, types, held, weights_here, own_ref)

    for first, weights in ((1, early), (1 + early.shape[0], late)):

        def table(level, carry, first=first, weights=weights):
            for kind in range(tables.shape[1]):
                put_weights(tables[first + level, kind], weights.at[level, kind])
            return carry

        lax.fori_loop(0, weights.shape[0], table, 0)

    def root(block, carry):
        hi, lo = split(maps[block])
        root_weights[block] = jnp.concatenate([hi, lo], axis=0)
        return carry

    lax.fori_loop(0, maps.shape[0], root, 0, unroll=4)


def middle_kernel(sources, types, weights, x_ref, other_ref, left_ref, held, held_too):
    blocks = held.shape[0]
    for pair in range(blocks // 2):
        put_pair(held, pair, x_ref[pair_rows(x_ref, pair), :])
    run_levels(1, 3, sources, types, (held, held_too), weights, flip_and_keep(left_ref, row_mask(3)))
    half_level(4, 2, blocks, sources, types, left_ref, weights.at[3], other_ref)


def own_kernel(sources, types, weights, left, own_ref):
    half_level(4, 0, 0, sources, types, left, weights.at[0], own_ref)


def end_kernel(sources, types, weights, own_ref, other_ref, out_ref, held, held_too):
    for pair in range(held.shape[0] // 2):
        rows = pair_rows(own_ref, pair)
        put_pair(held, pair, own_ref[rows, :] + other_ref[rows, :])
    run_levels(5, 3, sources, types, (held, held_too), weights, flip_and_give(out_ref, row_mask(7)))


def root_kernel(x_ref, weights, out_ref):
    blocks, rank, width = weights.shape[0], weights.shape[1] // 2, weights.shape[2]

    def body(pair, carry):
        x = x_ref[pair_rows(x_ref, pair), :]
        turned = turn(x)
        low = low_lanes(x.shape)
        for block, value in ((2 * pair, jnp.where(low, x, turned)), (2 * pair + 1, jnp.where(low, turned, x))):
            left = hi_lo_lanes(value)
            hi, lo = weights[block, :rank], weights[block, rank:]
            right = jnp.concatenate([hi, hi, lo, lo], axis=0)
            out = jnp.dot(jnp.concatenate([left, left], axis=1), right, preferred_element_type=F32)
            out_ref[:, pl.ds(pl.multiple_of(block * width, width), width)] = out
        return carry

    lax.fori_loop(0, blocks // 2, body, 0, unroll=True)


VMEM = pl.BlockSpec(memory_space=pltpu.VMEM)
SMEM = pl.BlockSpec(memory_space=pltpu.SMEM)
HBM = pl.BlockSpec(memory_space=pltpu.HBM)


def call(kernel, outs, specs, scratch=(), mib=12, cost=None):
    return pl.pallas_call(
        kernel,
        out_shape=outs,
        grid=(1,),
        in_specs=specs,
        out_specs=[VMEM] * len(outs),
        scratch_shapes=scratch,
        cost_estimate=cost,
        compiler_params=pltpu.CompilerParams(vmem_limit_bytes=mib * 2**20),
    )


def exchange(x):
    rows = x.shape[0]
    x = x.reshape(64, 1, rows * LANES // 64)
    return lax.all_to_all(x, GROUP, 0, 0, tiled=True).reshape(rows, LANES)


def partner(x, axis):
    return lax.ppermute(x, axis, [(0, 1), (1, 0)])


def local(signals, leaf_maps, root_maps, translations, source_list, type_list):
    blocks, rank, width = leaf_maps.shape
    waves = signals.shape[0]
    levels, kinds = translations.shape[:2]
    sources, types = jnp.swapaxes(source_list, 1, 2), jnp.swapaxes(type_list, 1, 2)
    root_maps = jnp.swapaxes(root_maps, 1, 2)
    held = pltpu.VMEM((blocks, waves, LANES), BF16)
    flat = jax.ShapeDtypeStruct((waves * blocks // 2, LANES), F32)
    other, left = call(
        start_kernel,
        [flat, jax.ShapeDtypeStruct((blocks, waves, LANES), BF16)],
        [SMEM, SMEM, HBM, HBM, HBM],
        [
            pltpu.VMEM((kinds, rank, LANES), BF16),
            pltpu.VMEM((kinds, rank, rank), F32),
            pltpu.VMEM((waves, blocks * width), F32),
            pltpu.VMEM((blocks, rank, width), F32),
            pltpu.SemaphoreType.DMA((3, 6)),
        ],
        mib=60,
    )(sources, types, translations, signals, leaf_maps)
    other, translations, root_maps = lax.optimization_barrier((other, translations, root_maps))
    received = partner(other, "y0")

    def prepared(count):
        return jax.ShapeDtypeStruct((count, kinds, rank, LANES), BF16)

    own, early, late, root_weights = call(
        prepare_kernel,
        [flat, prepared(4), prepared(3), jax.ShapeDtypeStruct((blocks, 2 * rank, width), BF16)],
        [SMEM, SMEM, VMEM, VMEM, VMEM],
        [pltpu.VMEM((kinds, rank, LANES), BF16)],
        cost=pl.CostEstimate(flops=2**24, bytes_accessed=2**23, transcendentals=0),
    )(sources, types, translations, root_maps, left)
    x, early, late, root_weights = lax.optimization_barrier((own + received, early, late, root_weights))
    x = exchange(x)
    other, left = call(
        middle_kernel,
        [flat, jax.ShapeDtypeStruct((blocks, waves, LANES), BF16)],
        [SMEM, SMEM, VMEM, VMEM],
        [held, held],
    )(sources, types, early, x)
    received = partner(other, "c")
    (own,) = call(
        own_kernel,
        [flat],
        [SMEM, SMEM, pl.BlockSpec((1, kinds, rank, LANES), lambda i: (3, 0, 0, 0)), VMEM],
        cost=pl.CostEstimate(flops=2**24, bytes_accessed=2**20, transcendentals=0),
    )(sources, types, early, left)
    (x,) = call(end_kernel, [flat], [SMEM, SMEM, VMEM, VMEM, VMEM], [held, held])(sources, types, late, own, received)
    (out,) = call(root_kernel, [jax.ShapeDtypeStruct((waves, blocks * width), F32)], [VMEM, VMEM])(
        exchange(x), root_weights
    )
    return out


def solution(mesh):
    fine = Mesh(mesh.devices.reshape((2,) * len(BITS)), BITS)
    placed = (P(None, BITS), P(BITS, None, None), P(BITS, None, None), P(), P(), P())
    return jax.shard_map(local, mesh=fine, in_specs=placed, out_specs=P(None, BITS), check_vma=False)
```
